128 devices in a mesh: req: 32 (over y, x, core), tp: 4 (over z).
Axes of the slice: x: 4, y: 4, z: 4, core: 2. Of those that a mesh axis runs over, the one named last changes fastest.
Arguments:
- tokens: bfloat16 [256, 2048], P('req'), may hold values from -6 to 6
- first_gain: float32 [2048], replicated, may hold values from 0.1 to 1.9
- query_weight: bfloat16 [2048, 2048], P(None, 'tp'), may hold values from -0.125 to 0.125
- key_weight: bfloat16 [2048, 2048], P(None, 'tp'), may hold values from -0.125 to 0.125
- value_weight: bfloat16 [2048, 2048], P(None, 'tp'), may hold values from -0.125 to 0.125
- out_weight: bfloat16 [2048, 2048], P('tp'), may hold values from -0.125 to 0.125
- second_gain: float32 [2048], replicated, may hold values from 0.1 to 1.9
- up_weight: bfloat16 [2048, 8192], P(None, ('req', 'tp')), may hold values from -0.125 to 0.125
- down_weight: bfloat16 [8192, 2048], P(('req', 'tp')), may hold values from -0.0625 to 0.0625
- cache_keys: bfloat16 [131072, 2048], P('req', 'tp'), may hold values from -480 to 480
- cache_values: bfloat16 [131072, 2048], P('req', 'tp'), may hold values from -6 to 6
- lengths: int32 [256], replicated, may hold values from 1 to 8192, 131072 in all
- stream_order: int32 [256], replicated, may hold values from 0 to 255, each once
Outputs:
- hidden: bfloat16 [256, 2048], P('req', 'tp')
- new_keys: bfloat16 [256, 2048], P('req', 'tp')
- new_values: bfloat16 [256, 2048], P('req', 'tp')
The draws below stay inside these ranges and needn't reach their ends.
Inputs may be any that keep to these rules, and one draw needn't show every extreme that they name: Every request's cache holds at least one row; the lengths sum to 131072 and the longest is exactly 8192. `stream_order`: each request appears exactly once.
All inputs are finite; a program needn't handle non-finite values.
Results may differ from the reference program's by a relative error of at most 0.0055.
The reference program's roundings to bfloat16 on the way (of `normed`, `queries`, `weights`, `attended`, `normed_two` and `activation`) count: a program that leaves them out, or rounds other values in their place, can miss the bound.
Values may be sent and summed in bfloat16 or wider, within the bound.
A program may use at most 128 MiB of HBM per device.

```python
import math
import jax
import jax.numpy as jnp
import numpy as np
from jax import lax

D = 2048
HEADS = 16
HEAD_DIM = 128
FF = 8192
ROWS_DEV = 4096
REQS = 256
TOTAL = 131072
MOST = 8192
N_REQ = 32


def draw_cache_keys(key, part):
    base = jnp.clip(jax.random.normal(key, (TOTAL, D), jnp.float32), -4.0, 4.0)
    return base.astype(jnp.bfloat16)


def level_of(stream_key, extent, pieces, low, largest):
    def one(position, blocks):
        steps = jax.random.uniform(jax.random.fold_in(jax.random.fold_in(stream_key, 6), position), (blocks,), jnp.float32, low / len(pieces), largest / len(pieces))
        return jnp.repeat(jnp.exp(steps), extent[position] // blocks).reshape((-1,) + (1,) * (len(extent) - position - 1))

    level = one(*pieces[0])
    for cut in pieces[1:]:
        level = level * one(*cut)
    return level


def profile(amount, total, reach, slope):
    weights = [(1 << 20) // math.isqrt(rank ** slope) + 1 for rank in range(2, amount + 1)]
    rest, holding = total - reach - (amount - 1), [1] * (amount - 1)
    while rest > 0:
        candidates = [i for i in range(amount - 1) if holding[i] < reach]
        pool, budget = sum([weights[i] for i in candidates]), rest
        for i in candidates:
            more = min(reach - holding[i], max(1, budget * weights[i] // pool), rest)
            holding[i] = holding[i] + more
            rest = rest - more
    return np.array([reach] + holding)


def ragged(stream_key, number_of, total, bound, skew):
    if number_of == 2:
        one = jax.random.randint(stream_key, (), max(1, total - bound), min(bound, total - 1) + 1)
        return jnp.stack([one, total - one])
    sizes = jnp.asarray(profile(number_of, total, bound, skew), jnp.int32)
    couples = (number_of - 1) // 2
    donor, taker = sizes[1:1 + 2 * couples:2], sizes[2:2 + 2 * couples:2]
    slack = jnp.minimum(donor - 1, bound - taker)
    moved = jax.random.randint(jax.random.fold_in(stream_key, 1), (couples,), 0, 1 << 20) % (slack + 1)
    sizes = sizes.at[1:1 + 2 * couples:2].set(donor - moved).at[2:2 + 2 * couples:2].set(taker + moved)
    return sizes[jax.random.permutation(jax.random.fold_in(stream_key, 2), number_of)]


def gaussian(stream_key, shape, width, bound, pieces=(), held_as=jnp.bfloat16):
    entries = jax.random.normal(stream_key, shape, jnp.float32) * width
    if len(pieces) > 0:
        entries = level_of(stream_key, shape, pieces, -0.22, 0.18) * entries
    return jnp.clip(entries, min=-bound, max=bound).astype(held_as)


def setup_inputs(seed: int = 0) -> dict:
    key_list = jax.random.split(jax.random.key(seed), 14)
    tokens = gaussian(key_list[0], (REQS, D), 1.0, 6.0, ((0, 32),))
    first_gain = jnp.clip(1.0 + 0.18 * jax.random.normal(key_list[1], (D,), jnp.float32), 0.1, 1.9)
    query_weight = gaussian(key_list[2], (D, D), D ** -0.5, 0.125, ((1, 4),))
    key_weight = gaussian(key_list[3], (D, D), D ** -0.5, 0.125, ((1, 4),))
    value_weight = gaussian(key_list[4], (D, D), D ** -0.5, 0.125, ((1, 4),))
    out_weight = gaussian(key_list[5], (D, D), D ** -0.5, 0.125, ((0, 4),))
    second_gain = jnp.clip(1.0 + 0.18 * jax.random.normal(key_list[6], (D,), jnp.float32), 0.1, 1.9)
    up_weight = gaussian(key_list[7], (D, FF), D ** -0.5, 0.125, ((1, 128),))
    down_weight = gaussian(key_list[8], (FF, D), FF ** -0.5, 0.0625, ((0, 128),))
    cache_keys = draw_cache_keys(jax.random.fold_in(key_list[13], 71), 0)
    cache_values = gaussian(key_list[10], (TOTAL, D), 1.0, 6.0, ((0, 32), (1, 4)))
    lengths = ragged(key_list[11], REQS, TOTAL, MOST, 2).astype(jnp.int32)
    stream_order = jax.random.permutation(key_list[12], REQS).astype(jnp.int32)
    return {"tokens": tokens, "first_gain": first_gain, "query_weight": query_weight, "key_weight": key_weight, "value_weight": value_weight, "out_weight": out_weight, "second_gain": second_gain, "up_weight": up_weight, "down_weight": down_weight, "cache_keys": cache_keys, "cache_values": cache_values, "lengths": lengths, "stream_order": stream_order}


def layer_norm(values, gain_vector):
    center = lax.optimization_barrier(jnp.mean(values, axis=-1, keepdims=True))
    shifted = values - center
    spread = lax.optimization_barrier(jnp.mean(shifted * shifted, axis=-1, keepdims=True))
    return shifted * lax.rsqrt(spread + 1e-05) * gain_vector

def reference(tokens, first_gain, query_weight, key_weight, value_weight, out_weight, second_gain, up_weight, down_weight, cache_keys, cache_values, lengths, stream_order):
    residual = tokens.astype(jnp.float32)
    normed = layer_norm(residual, first_gain).astype(jnp.bfloat16)
    queries = (jnp.dot(normed, query_weight, preferred_element_type=jnp.float32) * HEAD_DIM ** (-0.5)).astype(jnp.bfloat16)
    new_keys = jnp.dot(normed, key_weight, preferred_element_type=jnp.float32).astype(jnp.bfloat16)
    new_values = jnp.dot(normed, value_weight, preferred_element_type=jnp.float32).astype(jnp.bfloat16)
    stream_len = jnp.take(lengths, stream_order).astype(jnp.int32)
    bounds = jnp.cumsum(stream_len).astype(jnp.int32)
    positions = jnp.arange(TOTAL, dtype=jnp.int32)
    slots = jnp.searchsorted(bounds, positions, side='right').astype(jnp.int32)
    row_owner = jnp.take(stream_order, slots).astype(jnp.int32)
    key_blocks = cache_keys.reshape(N_REQ, ROWS_DEV, D)
    value_blocks = cache_values.reshape(N_REQ, ROWS_DEV, D)
    owner_blocks = row_owner.reshape(N_REQ, ROWS_DEV)

    def one_block(items):
        block_keys, block_values, block_owner = items
        row_query = jnp.take(queries, block_owner, axis=0).astype(jnp.float32).reshape(ROWS_DEV, HEADS, HEAD_DIM)
        scores = lax.optimization_barrier(jnp.sum(row_query * block_keys.astype(jnp.float32).reshape(ROWS_DEV, HEADS, HEAD_DIM), axis=-1))
        peak = jnp.maximum(jax.ops.segment_max(scores, block_owner, num_segments=REQS), -1e+30)
        expo = jnp.exp(scores - jnp.take(peak, block_owner, axis=0))
        mass = jax.ops.segment_sum(expo, block_owner, num_segments=REQS)
        weights = expo.astype(jnp.bfloat16)
        weighted = weights.astype(jnp.float32)[:, :, None] * block_values.astype(jnp.float32).reshape(ROWS_DEV, HEADS, HEAD_DIM)
        partial_value = jax.ops.segment_sum(weighted, block_owner, num_segments=REQS)
        return (peak, mass, partial_value)
    peaks, masses, partials = lax.map(one_block, (key_blocks, value_blocks, owner_blocks))
    self_score = lax.optimization_barrier(jnp.sum(queries.astype(jnp.float32).reshape(REQS, HEADS, HEAD_DIM) * new_keys.astype(jnp.float32).reshape(REQS, HEADS, HEAD_DIM), axis=-1))
    ceiling = jnp.maximum(lax.optimization_barrier(jnp.max(peaks, axis=0)), self_score)
    block_scale = jnp.exp(peaks - ceiling[None])
    self_weight = jnp.exp(self_score - ceiling)
    total = self_weight + lax.optimization_barrier(jnp.sum(masses * block_scale, axis=0))
    summed = self_weight[:, :, None] * new_values.astype(jnp.float32).reshape(REQS, HEADS, HEAD_DIM)
    summed = summed + lax.optimization_barrier(jnp.sum(partials * block_scale[:, :, :, None], axis=0))
    attended = (summed / total[:, :, None]).reshape(REQS, D).astype(jnp.bfloat16)
    middle = residual + jnp.dot(attended, out_weight, preferred_element_type=jnp.float32)
    normed_two = layer_norm(middle, second_gain).astype(jnp.bfloat16)
    activation = jax.nn.gelu(jnp.dot(normed_two, up_weight, preferred_element_type=jnp.float32), approximate=False).astype(jnp.bfloat16)
    hidden = (middle + jnp.dot(activation, down_weight, preferred_element_type=jnp.float32)).astype(jnp.bfloat16)
    return (hidden, new_keys, new_values)
```

```python
import functools

import jax
import jax.numpy as jnp
from jax import lax
from jax.experimental import pallas as pl
from jax.experimental.pallas import tpu as pltpu
from jax.sharding import PartitionSpec as P

HEAD = 128
MESH = pl.DeviceIdType.MESH
NEG = -1e30
WIN = 32
CHUNK = 512
NT = (((1,), (1,)), ((), ()))


def norm(v, g):
    center = jnp.mean(v, axis=-1, keepdims=True)
    shifted = v - center
    spread = jnp.mean(shifted * shifted, axis=-1, keepdims=True)
    return shifted * lax.rsqrt(spread + 1e-05) * g


def dot(a, b):
    return jnp.dot(a, b, preferred_element_type=jnp.float32)


def each(lo, hi, f):
    def step(i, carry):
        f(i)
        return carry

    lax.fori_loop(lo, hi, step, 0)


def project(n, tok, gain, lens, order, wq, wk, wv, q_all, nk, nv, tab, wb, qs, wsem, ss, rs):
    me, z = lax.axis_index("req"), lax.axis_index("tp")
    part = wq.shape[0] // 4
    loads = [
        pltpu.make_async_copy(
            wq.at[pl.ds(i * part, part)], wb.at[0, pl.ds(i * part, part)], wsem.at[i]
        )
        for i in range(4)
    ]
    loads += [
        pltpu.make_async_copy(wk, wb.at[1], wsem.at[4]),
        pltpu.make_async_copy(wv, wb.at[2], wsem.at[5]),
    ]
    for load in loads:
        load.start()
    barrier = pltpu.get_barrier_semaphore()

    def greet(d):
        peer = lax.rem(me + d, n)
        pl.semaphore_signal(barrier, inc=1, device_id=(peer, z), device_id_type=MESH)

    each(1, n, greet)
    normed = norm(tok[...].astype(jnp.float32), gain[...]).astype(jnp.bfloat16)
    q = jnp.zeros((tok.shape[0], wq.shape[1]), jnp.float32)
    for i in range(4):
        loads[i].wait()
        q += dot(normed[:, i * part : (i + 1) * part], wb[0, i * part : (i + 1) * part])
    q = (q * HEAD**-0.5).astype(jnp.bfloat16)
    qs[...] = q
    q_all[me] = q
    pl.semaphore_wait(barrier, n - 1)

    def send(d):
        peer = lax.rem(me + d, n)
        pltpu.make_async_remote_copy(
            qs, q_all.at[me], ss.at[d], rs.at[me], device_id=(peer, z), device_id_type=MESH
        ).start()

    each(1, n, send)
    loads[4].wait()
    nk[...] = dot(normed, wb[1]).astype(jnp.bfloat16)
    loads[5].wait()
    nv[...] = dot(normed, wb[2]).astype(jnp.bfloat16)
    m = lens.shape[1]
    sub = lax.broadcasted_iota(jnp.int32, (m, m), 0).astype(jnp.float32)
    lane = lax.broadcasted_iota(jnp.int32, (m, m), 1).astype(jnp.float32)
    len_l = lens[...].astype(jnp.float32)
    ord_s = jnp.sum(
        jnp.where(sub == lane, order[...].astype(jnp.float32), 0.0), axis=1, keepdims=True
    )
    hot = ord_s == lane
    rank = jnp.sum(jnp.where(hot, sub, 0.0), axis=0, keepdims=True)
    len_s = jnp.sum(jnp.where(hot, len_l, 0.0), axis=1, keepdims=True)
    end = jnp.sum(jnp.where(sub <= rank, len_s, 0.0), axis=0, keepdims=True)
    tab[0:1] = rank
    tab[1:2] = end - len_l
    tab[2:3] = end
    tab[3:8] = jnp.zeros((5, m), jnp.float32)

    def finish(d):
        src = lax.rem(me + d, n)
        copy = pltpu.make_async_remote_copy(
            qs, q_all.at[src], ss.at[d], rs.at[src], device_id=(src, z), device_id_type=MESH
        )
        copy.wait_recv()
        copy.wait_send()

    each(1, n, finish)


def attend(q_all, tab, nk_in, nv_in, keys, values, part, nk, nv, kb, vb, sc, acc, ksem, vsem):
    rows, width = keys.shape
    heads = width // HEAD
    steps = rows // CHUNK
    span = lambda i: pl.ds(i * CHUNK, CHUNK)
    kl = [pltpu.make_async_copy(keys.at[span(i)], kb.at[span(i)], ksem.at[i]) for i in range(steps)]
    vl = [
        pltpu.make_async_copy(values.at[span(i)], vb.at[span(i)], vsem.at[i]) for i in range(steps)
    ]
    for load in kl + vl:
        load.start()
    nk[...] = nk_in[...]
    nv[...] = nv_in[...]
    base = lax.axis_index("req") * rows
    base_f = base.astype(jnp.float32)
    rank, first, end = tab[0:1], tab[1:2], tab[2:3]
    m = rank.shape[1]
    sub = lax.broadcasted_iota(jnp.int32, (m, m), 0)
    lane = lax.broadcasted_iota(jnp.int32, (m, m), 1)
    diag = sub == lane
    upright = lambda row: jnp.sum(jnp.where(diag, row, 0.0), axis=1, keepdims=True)
    rank_s = upright(rank)
    here = jnp.logical_and(first < base_f + rows, end > base_f)
    here_s = upright(jnp.where(here, 1.0, 0.0)) > 0.5
    low = jnp.min(jnp.where(here, rank, 1e9)).astype(jnp.int32)
    high = jnp.max(jnp.where(here, rank, -1.0)).astype(jnp.int32)
    every_q = q_all[...].astype(jnp.float32).reshape(m, width).astype(jnp.bfloat16)
    tall = WIN * heads
    block = (
        lax.broadcasted_iota(jnp.int32, (tall, width), 0) // WIN
        == lax.broadcasted_iota(jnp.int32, (tall, width), 1) // HEAD
    )
    spot = lax.broadcasted_iota(jnp.int32, (WIN, HEAD), 1)

    def window(slot, opening):
        slot_f = slot.astype(jnp.float32)
        pick = rank == slot_f + lax.broadcasted_iota(jnp.int32, (WIN, m), 0).astype(jnp.float32)
        pick_f = jnp.where(pick, 1.0, 0.0)
        q = dot(pick_f.astype(jnp.bfloat16), every_q)
        first_w = jnp.sum(pick_f * first, axis=1, keepdims=True) - base_f
        end_w = jnp.sum(pick_f * end, axis=1, keepdims=True) - base_f
        first_t = jnp.concatenate([first_w] * heads, axis=0)
        end_t = jnp.concatenate([end_w] * heads, axis=0)
        q_block = jnp.where(block, jnp.concatenate([q] * heads, axis=0), 0.0).astype(jnp.bfloat16)
        top = jnp.full((tall, HEAD), NEG, jnp.float32)
        for i in range(steps):
            if opening:
                kl[i].wait()
            s = lax.dot_general(
                q_block, kb[i * CHUNK : (i + 1) * CHUNK], NT, preferred_element_type=jnp.float32
            )
            at = lax.broadcasted_iota(jnp.int32, (tall, CHUNK), 1).astype(jnp.float32) + float(
                i * CHUNK
            )
            s = jnp.where(jnp.logical_and(at >= first_t, at < end_t), s, NEG)
            sc[:, i * CHUNK : (i + 1) * CHUNK] = s
            for j in range(CHUNK // HEAD):
                top = jnp.maximum(top, s[:, j * HEAD : (j + 1) * HEAD])
        peak = jnp.max(top, axis=1, keepdims=True)
        held = jnp.zeros((tall, HEAD), jnp.float32)
        for i in range(steps):
            if opening:
                vl[i].wait()
            s = sc[:, i * CHUNK : (i + 1) * CHUNK]
            e = jnp.where(s > 0.1 * NEG, jnp.exp(s - peak), 0.0)
            for j in range(CHUNK // HEAD):
                held += e[:, j * HEAD : (j + 1) * HEAD]
            o = dot(e.astype(jnp.bfloat16), vb[i * CHUNK : (i + 1) * CHUNK])
            if i == 0:
                acc[...] = o
            else:
                acc[...] += o
        mass = jnp.sum(held, axis=1, keepdims=True)
        cut = lambda a, h: a[h * WIN : (h + 1) * WIN]
        stat = jnp.zeros((WIN, HEAD), jnp.float32)
        for h in range(heads):
            stat = jnp.where(spot == h, cut(peak, h), stat)
            stat = jnp.where(spot == heads + h, cut(mass, h), stat)
        found = jnp.concatenate(
            [
                acc[h * WIN : (h + 1) * WIN, h * HEAD : (h + 1) * HEAD] for h in range(heads)
            ]
            + [stat],
            axis=1,
        )
        put = rank_s == slot_f + lax.broadcasted_iota(jnp.int32, (m, WIN), 1).astype(jnp.float32)
        put = jnp.where(put, 1.0, 0.0).astype(jnp.bfloat16)
        one = found.astype(jnp.bfloat16)
        rest = found - one.astype(jnp.float32)
        two = rest.astype(jnp.bfloat16)
        three = (rest - two.astype(jnp.float32)).astype(jnp.bfloat16)
        placed = (dot(put, one) + dot(put, two)) + dot(put, three)
        if opening:
            part[...] = placed
        else:
            part[...] += placed

    window(low, True)
    each(1, (high - low) // WIN + 1, lambda w: window(low + w * WIN, False))
    stat = part[:, width:]
    lanes = lax.broadcasted_iota(jnp.int32, stat.shape, 1)
    part[:, width:] = jnp.where(
        jnp.logical_and(lanes < heads, jnp.logical_not(here_s)), NEG, stat
    )


def tail(
    n, t, nx, part, q_all, nk, nv, tok, gain, wo, up, down, hid,
    got, wob, upb, dnb, zs, zr, mc, ns, nr, ts, rr,
    lsem, a_s, a_r, u_s, u_r, d_s, d_r, z_s, z_r, n_s, n_r, r_s, r_r,
):
    me, z = lax.axis_index("req"), lax.axis_index("tp")
    ny = n // (2 * nx)
    y, x, c = me // (2 * nx), lax.rem(me // 2, nx), lax.rem(me, 2)
    nj = 2 * ny
    j0 = y * 2 + c
    k0 = j0 * t + z
    nk0 = nj * t
    width = q_all.shape[2]
    heads = width // HEAD
    own = tok.shape[0]

    def home(j):
        return ((j // 2) * nx + x) * 2 + lax.rem(j, 2)

    loads = [
        pltpu.make_async_copy(wo, wob, lsem.at[0]),
        pltpu.make_async_copy(up, upb.at[x], lsem.at[1]),
        pltpu.make_async_copy(down, dnb.at[x], lsem.at[2]),
        pltpu.make_async_copy(part.at[me], got.at[me], lsem.at[3]),
    ]
    for load in loads:
        load.start()
    barrier = pltpu.get_barrier_semaphore()

    def greet(d):
        peer = lax.rem(me + d, n)
        pl.semaphore_signal(barrier, inc=1, device_id=(peer, z), device_id_type=MESH)

    each(1, n, greet)

    def greet_plane(i):
        pz = lax.rem(z + 1 + i // nj, t)
        pl.semaphore_signal(
            barrier, inc=1, device_id=(home(lax.rem(i, nj)), pz), device_id_type=MESH
        )

    each(0, nj * (t - 1), greet_plane)
    pl.semaphore_wait(barrier, n - 1 + nj * (t - 1))

    def partial_copy(d, src, peer):
        return pltpu.make_async_remote_copy(
            part.at[peer], got.at[src], a_s.at[d], a_r.at[src],
            device_id=(peer, z), device_id_type=MESH,
        )

    each(1, n, lambda d: partial_copy(d, me, lax.rem(me + d, n)).start())

    def weight_copies(d, src):
        peer = (y * nx + lax.rem(x + d, nx)) * 2 + c
        return [
            pltpu.make_async_remote_copy(
                up, upb.at[src], u_s.at[d], u_r.at[src], device_id=(peer, z), device_id_type=MESH
            ),
            pltpu.make_async_remote_copy(
                down, dnb.at[src], d_s.at[d], d_r.at[src], device_id=(peer, z), device_id_type=MESH
            ),
        ]

    def weights_out(d):
        for copy in weight_copies(d, x):
            copy.start()

    each(1, nx, weights_out)

    q = q_all[me].astype(jnp.float32)
    kn = nk[...].astype(jnp.float32)
    vn = nv[...].astype(jnp.float32)
    spot = lax.broadcasted_iota(jnp.int32, (own, HEAD), 1)
    mine = jnp.zeros((own, HEAD), jnp.float32)
    for h in range(heads):
        cols = slice(h * HEAD, (h + 1) * HEAD)
        mine = jnp.where(spot == h, jnp.sum(q[:, cols] * kn[:, cols], axis=1, keepdims=True), mine)
    loads[3].wait()

    def partial_in(d):
        copy = partial_copy(d, lax.rem(me + d, n), lax.rem(me + d, n))
        copy.wait_recv()
        copy.wait_send()

    each(1, n, partial_in)
    stat = got[:, :, width:]
    top = jnp.maximum(jnp.max(stat, axis=0), mine)
    scale = jnp.exp(stat - top[None])
    mass = pltpu.roll(stat, HEAD - heads, axis=2)
    self_w = jnp.exp(mine - top)
    total = self_w + jnp.sum(scale * mass, axis=0)
    pieces = []
    for h in range(heads):
        cols = slice(h * HEAD, (h + 1) * HEAD)
        older = jnp.sum(got[:, :, cols] * scale[:, :, h : h + 1], axis=0)
        pieces.append((self_w[:, h : h + 1] * vn[:, cols] + older) / total[:, h : h + 1])
    attended = jnp.concatenate(pieces, axis=1).astype(jnp.bfloat16)
    loads[0].wait()
    pm = dot(attended, wob[...])
    zs[...] = pm
    zr[z] = pm

    def middle_copy(d, src):
        return pltpu.make_async_remote_copy(
            zs, zr.at[src], z_s.at[d], z_r.at[src],
            device_id=(me, lax.rem(z + d, t)), device_id_type=MESH,
        )

    each(1, t, lambda d: middle_copy(d, z).start())

    def middle_in(d):
        copy = middle_copy(d, lax.rem(z + d, t))
        copy.wait_recv()
        copy.wait_send()

    each(1, t, middle_in)
    mid = zr[0]
    for i in range(1, t):
        mid += zr[i]
    mid += tok[...].astype(jnp.float32)
    for i in range(t):
        mc[i] = mid[:, i * width : (i + 1) * width]
    normed = norm(mid, gain[...]).astype(jnp.bfloat16)
    ns[...] = normed
    nr[j0] = normed

    def normed_copy(d, src):
        return pltpu.make_async_remote_copy(
            ns, nr.at[src], n_s.at[d], n_r.at[src],
            device_id=(home(lax.rem(j0 + d, nj)), z), device_id_type=MESH,
        )

    each(1, nj, lambda d: normed_copy(d, j0).start())

    def normed_in(d):
        copy = normed_copy(d, lax.rem(j0 + d, nj))
        copy.wait_recv()
        copy.wait_send()

    each(1, nj, normed_in)
    loads[1].wait()
    loads[2].wait()

    def weights_in(d):
        for copy in weight_copies(d, lax.rem(x + d, nx)):
            copy.wait_recv()
            copy.wait_send()

    each(1, nx, weights_in)
    tokens, units, wide = nj * own, nx * up.shape[0], up.shape[1]
    rows = nr[...].astype(jnp.float32).reshape(tokens, wide).astype(jnp.bfloat16)
    pre = lax.dot_general(
        rows, upb[...].reshape(units, wide), NT, preferred_element_type=jnp.float32
    )
    act = (0.5 * pre * (1.0 + lax.erf(pre * 0.5**0.5))).astype(jnp.bfloat16)
    for i in range(t):
        cols = slice(i * width, (i + 1) * width)
        term = dot(act, dnb[:, :, cols].reshape(units, width))
        ts[:, i] = term.reshape(nj, own, width)
    rr[k0] = ts[j0, z]

    def term_copy(d, src):
        k = lax.rem(k0 + d, nk0)
        return pltpu.make_async_remote_copy(
            ts.at[k // t, lax.rem(k, t)], rr.at[src], r_s.at[d], r_r.at[src],
            device_id=(home(k // t), lax.rem(k, t)), device_id_type=MESH,
        )

    each(1, nk0, lambda d: term_copy(d, k0).start())

    def term_in(d):
        copy = term_copy(d, lax.rem(k0 + d, nk0))
        copy.wait_recv()
        copy.wait_send()

    each(1, nk0, term_in)
    hid[...] = (mc[z] + jnp.sum(rr[...], axis=0)).astype(jnp.bfloat16)


def body(
    n, t, nx, tokens, first_gain, query_weight, key_weight, value_weight, out_weight, second_gain,
    up_weight, down_weight, cache_keys, cache_values, lengths, stream_order,
):
    f32, b16 = jnp.float32, jnp.bfloat16
    own, wide = tokens.shape
    width = query_weight.shape[1]
    requests = own * n
    units = up_weight.shape[1]
    rows = cache_keys.shape[0]
    steps = rows // CHUNK
    vmem = pl.BlockSpec(memory_space=pltpu.VMEM)
    hbm = pl.BlockSpec(memory_space=pl.ANY)
    dma = pltpu.SemaphoreType.DMA
    shape = jax.ShapeDtypeStruct
    q_all, nk, nv, tab = pl.pallas_call(
        functools.partial(project, n),
        out_shape=(
            shape((n, own, width), b16),
            shape((own, width), b16),
            shape((own, width), b16),
            shape((8, requests), f32),
        ),
        in_specs=[vmem] * 4 + [hbm] * 3,
        out_specs=(vmem,) * 4,
        scratch_shapes=[
            pltpu.VMEM((3, wide, width), b16),
            pltpu.VMEM((own, width), b16),
            dma((6,)),
            dma((n,)),
            dma((n,)),
        ],
        compiler_params=pltpu.CompilerParams(collective_id=0, has_side_effects=True),
        name="project",
    )(
        tokens, first_gain.reshape(1, wide), lengths.reshape(1, requests),
        stream_order.reshape(1, requests), query_weight, key_weight, value_weight,
    )
    part, new_keys, new_values = pl.pallas_call(
        attend,
        out_shape=(
            shape((requests, width + HEAD), f32),
            shape((own, width), b16),
            shape((own, width), b16),
        ),
        in_specs=[vmem] * 4 + [hbm] * 2,
        out_specs=(vmem,) * 3,
        scratch_shapes=[
            pltpu.VMEM((rows, width), b16),
            pltpu.VMEM((rows, width), b16),
            pltpu.VMEM((WIN * width // HEAD, rows), f32),
            pltpu.VMEM((WIN * width // HEAD, width), f32),
            dma((steps,)),
            dma((steps,)),
        ],
        name="attend",
    )(q_all, tab, nk, nv, cache_keys, cache_values)
    nj = n // nx
    hidden = pl.pallas_call(
        functools.partial(tail, n, t, nx),
        out_shape=shape((own, width), b16),
        in_specs=[hbm] + [vmem] * 5 + [hbm] * 3,
        out_specs=vmem,
        scratch_shapes=[
            pltpu.VMEM((n, own, width + HEAD), f32),
            pltpu.VMEM((width, wide), b16),
            pltpu.VMEM((nx, units, wide), b16),
            pltpu.VMEM((nx, units, wide), b16),
            pltpu.VMEM((own, wide), f32),
            pltpu.VMEM((t, own, wide), f32),
            pltpu.VMEM((t, own, width), f32),
            pltpu.VMEM((own, wide), b16),
            pltpu.VMEM((nj, own, wide), b16),
            pltpu.VMEM((nj, t, own, width), f32),
            pltpu.VMEM((nj * t, own, width), f32),
            dma((4,)),
            dma((n,)), dma((n,)),
            dma((nx,)), dma((nx,)),
            dma((nx,)), dma((nx,)),
            dma((t,)), dma((t,)),
            dma((nj,)), dma((nj,)),
            dma((nj * t,)), dma((nj * t,)),
        ],
        compiler_params=pltpu.CompilerParams(collective_id=1, has_side_effects=True),
        name="tail",
    )(
        part.reshape(n, own, width + HEAD), q_all, new_keys, new_values, tokens,
        second_gain.reshape(1, wide), out_weight, up_weight.T, down_weight,
    )
    return hidden, new_keys, new_values


def solution(mesh):
    n, t = mesh.shape["req"], mesh.shape["tp"]
    return jax.shard_map(
        functools.partial(body, n, t, 4),
        mesh=mesh,
        in_specs=(
            P("req", None), P(), P(None, "tp"), P(None, "tp"), P(None, "tp"), P("tp", None), P(),
            P(None, ("req", "tp")), P(("req", "tp"), None), P("req", "tp"), P("req", "tp"), P(), P(),
        ),
        out_specs=(P("req", "tp"), P("req", "tp"), P("req", "tp")),
        check_vma=False,
    )
```

```python
import functools

import jax
import jax.numpy as jnp
from jax import lax
from jax.experimental import pallas as pl
from jax.experimental.pallas import tpu as pltpu
from jax.sharding import PartitionSpec as P

HEAD = 128
MESH = pl.DeviceIdType.MESH
NEG = -1e30
WIN = 32
CHUNK = 512
VMEM_PROJECT, VMEM_ATTEND, VMEM_TAIL = 20 << 20, 16 << 20, 16 << 20
NT = (((1,), (1,)), ((), ()))


def norm(v, g):
    center = jnp.mean(v, axis=-1, keepdims=True)
    shifted = v - center
    spread = jnp.mean(shifted * shifted, axis=-1, keepdims=True)
    return shifted * lax.rsqrt(spread + 1e-05) * g


def dot(a, b):
    return jnp.dot(a, b, preferred_element_type=jnp.float32)


def each(lo, hi, f):
    def step(i, carry):
        f(i)
        return carry

    lax.fori_loop(lo, hi, step, 0)


def project(
    n, nx, tok_h, gain_h, lens_h, order_h, wq, wk, wv, keys, values, up,
    q_all, nk, nv, tab, kb, vb, un,
    tok, gain, lens, order, wb, qs, wsem, ss, rs, us, ur,
):
    me, z = lax.axis_index("req"), lax.axis_index("tp")
    part = wq.shape[0] // 4
    small = [
        pltpu.make_async_copy(a, b, wsem.at[8 + i])
        for i, (a, b) in enumerate([(tok_h, tok), (gain_h, gain), (lens_h, lens), (order_h, order)])
    ]
    loads = [
        pltpu.make_async_copy(
            wq.at[pl.ds(i * part, part)], wb.at[0, pl.ds(i * part, part)], wsem.at[i]
        )
        for i in range(4)
    ]
    loads += [
        pltpu.make_async_copy(wk, wb.at[1], wsem.at[4]),
        pltpu.make_async_copy(wv, wb.at[2], wsem.at[5]),
        pltpu.make_async_copy(keys, kb, wsem.at[6]),
        pltpu.make_async_copy(values, vb, wsem.at[7]),
    ]
    for load in small + loads[:4]:
        load.start()
    barrier = pltpu.get_barrier_semaphore()

    def greet(d):
        peer = lax.rem(me + d, n)
        pl.semaphore_signal(barrier, inc=1, device_id=(peer, z), device_id_type=MESH)

    each(1, n, greet)
    small[0].wait()
    small[1].wait()
    normed = norm(tok[...].astype(jnp.float32), gain[...]).astype(jnp.bfloat16)
    q = jnp.zeros((tok.shape[0], wq.shape[1]), jnp.float32)
    for i in range(4):
        loads[i].wait()
        q += dot(normed[:, i * part : (i + 1) * part], wb[0, i * part : (i + 1) * part])
    for load in loads[4:]:
        load.start()
    q = (q * HEAD**-0.5).astype(jnp.bfloat16)
    qs[...] = q
    q_all[me] = q
    pl.semaphore_wait(barrier, n - 1)

    def send(d):
        peer = lax.rem(me + d, n)
        pltpu.make_async_remote_copy(
            qs, q_all.at[me], ss.at[d], rs.at[me], device_id=(peer, z), device_id_type=MESH
        ).start()

    each(1, n, send)
    sides = side_copies(up, un, us, ur, me, z, nx)
    for copy in sides:
        copy.start()
    loads[4].wait()
    nk[...] = dot(normed, wb[1]).astype(jnp.bfloat16)
    loads[5].wait()
    nv[...] = dot(normed, wb[2]).astype(jnp.bfloat16)
    small[2].wait()
    small[3].wait()
    m = lens.shape[1]
    sub = lax.broadcasted_iota(jnp.int32, (m, m), 0).astype(jnp.float32)
    lane = lax.broadcasted_iota(jnp.int32, (m, m), 1).astype(jnp.float32)
    len_l = lens[...].astype(jnp.float32)
    ord_s = jnp.sum(
        jnp.where(sub == lane, order[...].astype(jnp.float32), 0.0), axis=1, keepdims=True
    )
    hot = ord_s == lane
    rank = jnp.sum(jnp.where(hot, sub, 0.0), axis=0, keepdims=True)
    len_s = jnp.sum(jnp.where(hot, len_l, 0.0), axis=1, keepdims=True)
    end = jnp.sum(jnp.where(sub <= rank, len_s, 0.0), axis=0, keepdims=True)
    tab[0:1] = rank
    tab[1:2] = end - len_l
    tab[2:3] = end
    tab[3:8] = jnp.zeros((5, m), jnp.float32)

    def finish(d):
        src = lax.rem(me + d, n)
        copy = pltpu.make_async_remote_copy(
            qs, q_all.at[src], ss.at[d], rs.at[src], device_id=(src, z), device_id_type=MESH
        )
        copy.wait_recv()
        copy.wait_send()

    each(1, n, finish)
    loads[6].wait()
    loads[7].wait()
    for copy in sides:
        copy.wait()


def along(me, d, nx):
    x = lax.rem(me // 2, nx)
    return me + (lax.rem(x + d, nx) - x) * 2


def side_copies(src, dst, ss, rs, me, z, nx):
    return [
        pltpu.make_async_remote_copy(
            src, dst.at[i], ss.at[i], rs.at[i],
            device_id=(along(me, d, nx), z), device_id_type=MESH,
        )
        for i, d in enumerate((1, nx - 1))
    ]


def relay_copies(slots, dst, ss, rs, me, z, nx):
    half = dst.shape[0] // 2
    return [
        pltpu.make_async_remote_copy(
            slots.at[i, pl.ds(i * half, half)], dst.at[pl.ds(i * half, half)], ss.at[i], rs.at[i],
            device_id=(along(me, d, nx), z), device_id_type=MESH,
        )
        for i, d in enumerate((1, nx - 1))
    ]


def attend(q_all, tab, nk_in, nv_in, kb, vb, part, nk, nv, sc, acc, put_all):
    rows, width = kb.shape
    heads = width // HEAD
    steps = rows // CHUNK
    nk[...] = nk_in[...]
    nv[...] = nv_in[...]
    base = lax.axis_index("req") * rows
    base_f = base.astype(jnp.float32)
    rank, first, end = tab[0:1], tab[1:2], tab[2:3]
    m = rank.shape[1]
    sub = lax.broadcasted_iota(jnp.int32, (m, m), 0)
    lane = lax.broadcasted_iota(jnp.int32, (m, m), 1)
    diag = sub == lane
    upright = lambda row: jnp.sum(jnp.where(diag, row, 0.0), axis=1, keepdims=True)
    rank_s = upright(rank)
    here = jnp.logical_and(first < base_f + rows, end > base_f)
    here_s = upright(jnp.where(here, 1.0, 0.0)) > 0.5
    low = jnp.min(jnp.where(here, rank, 1e9)).astype(jnp.int32)
    high = jnp.max(jnp.where(here, rank, -1.0)).astype(jnp.int32)
    every_q = q_all[...].astype(jnp.float32).reshape(m, width).astype(jnp.bfloat16)
    tall = WIN * heads
    block = (
        lax.broadcasted_iota(jnp.int32, (tall, width), 0) // WIN
        == lax.broadcasted_iota(jnp.int32, (tall, width), 1) // HEAD
    )
    spot = lax.broadcasted_iota(jnp.int32, (WIN, HEAD), 1)

    def window(slot, opening):
        slot_f = slot.astype(jnp.float32)
        pick = rank == slot_f + lax.broadcasted_iota(jnp.int32, (WIN, m), 0).astype(jnp.float32)
        pick_f = jnp.where(pick, 1.0, 0.0)
        q = dot(pick_f.astype(jnp.bfloat16), every_q)
        first_w = jnp.sum(pick_f * first, axis=1, keepdims=True) - base_f
        end_w = jnp.sum(pick_f * end, axis=1, keepdims=True) - base_f
        first_t = jnp.concatenate([first_w] * heads, axis=0)
        end_t = jnp.concatenate([end_w] * heads, axis=0)
        q_block = jnp.where(block, jnp.concatenate([q] * heads, axis=0), 0.0).astype(jnp.bfloat16)
        top = jnp.full((tall, HEAD), NEG, jnp.float32)
        for i in range(steps):
            s = lax.dot_general(
                q_block, kb[i * CHUNK : (i + 1) * CHUNK], NT, preferred_element_type=jnp.float32
            )
            at = lax.broadcasted_iota(jnp.int32, (tall, CHUNK), 1).astype(jnp.float32) + float(
                i * CHUNK
            )
            s = jnp.where(jnp.logical_and(at >= first_t, at < end_t), s, NEG)
            sc[:, i * CHUNK : (i + 1) * CHUNK] = s
            for j in range(CHUNK // HEAD):
                top = jnp.maximum(top, s[:, j * HEAD : (j + 1) * HEAD])
        peak = jnp.max(top, axis=1, keepdims=True)
        held = jnp.zeros((tall, HEAD), jnp.float32)
        for i in range(steps):
            s = sc[:, i * CHUNK : (i + 1) * CHUNK]
            e = jnp.where(s > 0.1 * NEG, jnp.exp(s - peak), 0.0)
            for j in range(CHUNK // HEAD):
                held += e[:, j * HEAD : (j + 1) * HEAD]
            o = dot(e.astype(jnp.bfloat16), vb[i * CHUNK : (i + 1) * CHUNK])
            if i == 0:
                acc[...] = o
            else:
                acc[...] += o
        mass = jnp.sum(held, axis=1, keepdims=True)
        cut = lambda a, h: a[h * WIN : (h + 1) * WIN]
        stat = jnp.zeros((WIN, HEAD), jnp.float32)
        for h in range(heads):
            stat = jnp.where(spot == h, cut(peak, h), stat)
            stat = jnp.where(spot == heads + h, cut(mass, h), stat)
        found = jnp.concatenate(
            [
                acc[h * WIN : (h + 1) * WIN, h * HEAD : (h + 1) * HEAD] for h in range(heads)
            ]
            + [stat],
            axis=1,
        )
        put = rank_s == slot_f + lax.broadcasted_iota(jnp.int32, (m, WIN), 1).astype(jnp.float32)
        put = jnp.where(put, 1.0, 0.0).astype(jnp.bfloat16)
        one = found.astype(jnp.bfloat16)
        rest = found - one.astype(jnp.float32)
        two = rest.astype(jnp.bfloat16)
        three = (rest - two.astype(jnp.float32)).astype(jnp.bfloat16)
        placed = (dot(put, one) + dot(put, two)) + dot(put, three)
        if opening:
            put_all[...] = placed
        else:
            put_all[...] += placed

    window(low, True)
    each(1, (high - low) // WIN + 1, lambda w: window(low + w * WIN, False))
    stat = put_all[:, width:]
    lanes = lax.broadcasted_iota(jnp.int32, stat.shape, 1)
    stat = jnp.where(jnp.logical_and(lanes < heads, jnp.logical_not(here_s)), NEG, stat)
    one = stat.astype(jnp.bfloat16).astype(jnp.float32)
    two = (stat - one).astype(jnp.bfloat16).astype(jnp.float32)
    three = (stat - one) - two
    kinds = 2 * heads
    stat = jnp.where(
        lanes < kinds,
        one,
        jnp.where(
            lanes < 2 * kinds, pltpu.roll(two, kinds, axis=1), pltpu.roll(three, 2 * kinds, axis=1)
        ),
    )
    shape = part.shape
    part[:, :, :width] = put_all[:, :width].reshape(shape[0], shape[1], width).astype(part.dtype)
    part[:, :, width:] = stat.reshape(shape[0], shape[1], HEAD).astype(part.dtype)


def tail(
    n, t, nx, part, q_all, nk, nv, tok, gain, wo, up, un, down, hid,
    got, upb, dnb, zs, zr, mc, ns, nr, ts, rr,
    lsem, a_s, a_r, u_s, u_r, d_s, d_r, e_s, e_r, z_s, z_r, n_s, n_r, r_s, r_r,
):
    me, z = lax.axis_index("req"), lax.axis_index("tp")
    ny = n // (2 * nx)
    y, x, c = me // (2 * nx), lax.rem(me // 2, nx), lax.rem(me, 2)
    nj = 2 * ny
    j0 = y * 2 + c
    k0 = j0 * t + z
    nk0 = nj * t
    width = q_all.shape[2]
    heads = width // HEAD
    own = tok.shape[0]

    def home(j):
        return ((j // 2) * nx + x) * 2 + lax.rem(j, 2)

    loads = [
        pltpu.make_async_copy(up, upb.at[0], lsem.at[1]),
        pltpu.make_async_copy(down, dnb.at[0], lsem.at[2]),
        pltpu.make_async_copy(part.at[me], got.at[me], lsem.at[3]),
        pltpu.make_async_copy(un, upb.at[pl.ds(1, 2)], lsem.at[4]),
    ]
    for load in loads:
        load.start()
    barrier = pltpu.get_barrier_semaphore()

    def greet(d):
        peer = lax.rem(me + d, n)
        pl.semaphore_signal(barrier, inc=1, device_id=(peer, z), device_id_type=MESH)

    each(1, n, greet)

    def greet_plane(i):
        pz = lax.rem(z + 1 + i // nj, t)
        pl.semaphore_signal(
            barrier, inc=1, device_id=(home(lax.rem(i, nj)), pz), device_id_type=MESH
        )

    each(0, nj * (t - 1), greet_plane)
    pl.semaphore_wait(barrier, n - 1 + nj * (t - 1))

    def partial_copy(d, src, peer):
        return pltpu.make_async_remote_copy(
            part.at[peer], got.at[src], a_s.at[d], a_r.at[src],
            device_id=(peer, z), device_id_type=MESH,
        )

    each(1, n, lambda d: partial_copy(d, me, lax.rem(me + d, n)).start())

    q = q_all[me].astype(jnp.float32)
    kn = nk[...].astype(jnp.float32)
    vn = nv[...].astype(jnp.float32)
    spot = lax.broadcasted_iota(jnp.int32, (own, HEAD), 1)
    mine = jnp.zeros((own, HEAD), jnp.float32)
    for h in range(heads):
        cols = slice(h * HEAD, (h + 1) * HEAD)
        mine = jnp.where(spot == h, jnp.sum(q[:, cols] * kn[:, cols], axis=1, keepdims=True), mine)
    loads[2].wait()

    def partial_in(d):
        copy = partial_copy(d, lax.rem(me + d, n), lax.rem(me + d, n))
        copy.wait_recv()
        copy.wait_send()

    each(1, n, partial_in)
    down_side = side_copies(down, dnb.at[pl.ds(1, 2)], d_s, d_r, me, z, nx)
    up_relay = relay_copies(un, upb.at[3], u_s, u_r, me, z, nx)
    down_relay = relay_copies(dnb.at[pl.ds(1, 2)], dnb.at[3], e_s, e_r, me, z, nx)
    for copy in down_side + up_relay:
        copy.start()
    kinds = 2 * heads
    coded = got[:, :, width:].astype(jnp.float32)
    stat = (coded + pltpu.roll(coded, HEAD - kinds, axis=2)) + pltpu.roll(
        coded, HEAD - 2 * kinds, axis=2
    )
    top = jnp.maximum(jnp.max(stat, axis=0), mine)
    scale = jnp.exp(stat - top[None])
    mass = pltpu.roll(stat, HEAD - heads, axis=2)
    self_w = jnp.exp(mine - top)
    total = self_w + jnp.sum(scale * mass, axis=0)
    pieces = []
    for h in range(heads):
        cols = slice(h * HEAD, (h + 1) * HEAD)
        older = jnp.sum(got[:, :, cols].astype(jnp.float32) * scale[:, :, h : h + 1], axis=0)
        pieces.append((self_w[:, h : h + 1] * vn[:, cols] + older) / total[:, h : h + 1])
    attended = jnp.concatenate(pieces, axis=1).astype(jnp.bfloat16)
    pm = dot(attended, wo[...])
    zs[...] = pm.astype(zs.dtype)

    def middle_copy(d, src):
        return pltpu.make_async_remote_copy(
            zs, zr.at[src], z_s.at[d], z_r.at[src],
            device_id=(me, lax.rem(z + d, t)), device_id_type=MESH,
        )

    each(1, t, lambda d: middle_copy(d, z).start())

    def middle_in(d):
        copy = middle_copy(d, lax.rem(z + d, t))
        copy.wait_recv()
        copy.wait_send()

    each(1, t, middle_in)
    for i in range(1, t):
        pm += zr[lax.rem(z + i, t)].astype(jnp.float32)
    mid = tok[...].astype(jnp.float32) + pm
    for i in range(t):
        mc[i] = mid[:, i * width : (i + 1) * width]
    normed = norm(mid, gain[...]).astype(jnp.bfloat16)
    ns[...] = normed
    nr[j0] = normed

    def normed_copy(d, src):
        return pltpu.make_async_remote_copy(
            ns, nr.at[src], n_s.at[d], n_r.at[src],
            device_id=(home(lax.rem(j0 + d, nj)), z), device_id_type=MESH,
        )

    each(1, nj, lambda d: normed_copy(d, j0).start())
    for copy in down_side:
        copy.wait()
    for copy in down_relay:
        copy.start()

    def normed_in(d):
        copy = normed_copy(d, lax.rem(j0 + d, nj))
        copy.wait_recv()
        copy.wait_send()

    each(1, nj, normed_in)
    loads[0].wait()
    loads[3].wait()
    for copy in up_relay:
        copy.wait()
    tokens, units, wide = nj * own, nx * up.shape[0], up.shape[1]
    rows = nr[...].astype(jnp.float32).reshape(tokens, wide).astype(jnp.bfloat16)
    pre = lax.dot_general(
        rows, upb[...].reshape(units, wide), NT, preferred_element_type=jnp.float32
    )
    act = (0.5 * pre * (1.0 + lax.erf(pre * 0.5**0.5))).astype(jnp.bfloat16)
    loads[1].wait()
    for copy in down_relay:
        copy.wait()
    for i in range(t):
        cols = slice(i * width, (i + 1) * width)
        term = dot(act, dnb[:, :, cols].reshape(units, width))
        ts[:, i] = term.reshape(nj, own, width).astype(ts.dtype)
    rr[k0] = ts[j0, z]

    def term_copy(d, src):
        k = lax.rem(k0 + d, nk0)
        return pltpu.make_async_remote_copy(
            ts.at[k // t, lax.rem(k, t)], rr.at[src], r_s.at[d], r_r.at[src],
            device_id=(home(k // t), lax.rem(k, t)), device_id_type=MESH,
        )

    each(1, nk0, lambda d: term_copy(d, k0).start())

    def term_in(d):
        copy = term_copy(d, lax.rem(k0 + d, nk0))
        copy.wait_recv()
        copy.wait_send()

    each(1, nk0, term_in)
    hid[...] = (mc[z] + jnp.sum(rr[...].astype(jnp.float32), axis=0)).astype(jnp.bfloat16)


def body(
    n, t, nx, tokens, first_gain, query_weight, key_weight, value_weight, out_weight, second_gain,
    up_weight, down_weight, cache_keys, cache_values, lengths, stream_order,
):
    f32, b16 = jnp.float32, jnp.bfloat16
    own, wide = tokens.shape
    width = query_weight.shape[1]
    requests = own * n
    units = up_weight.shape[1]
    rows = cache_keys.shape[0]
    steps = rows // CHUNK
    vmem = pl.BlockSpec(memory_space=pltpu.VMEM)
    hbm = pl.BlockSpec(memory_space=pltpu.HBM)
    free = pl.BlockSpec(memory_space=pl.ANY)
    dma = pltpu.SemaphoreType.DMA
    shape = jax.ShapeDtypeStruct
    up_rows = up_weight.T
    held = lambda a: pltpu.with_memory_space_constraint(a, pltpu.HBM)
    heads = width // HEAD
    q_all, nk, nv, tab, kb, vb, un = pl.pallas_call(
        functools.partial(project, n, nx),
        out_shape=(
            shape((n, own, width), b16),
            shape((own, width), b16),
            shape((own, width), b16),
            shape((8, requests), f32),
            shape((rows, width), b16),
            shape((rows, width), b16),
            shape((2, units, wide), b16),
        ),
        in_specs=[hbm] * 10,
        out_specs=(vmem,) * 7,
        scratch_shapes=[
            pltpu.VMEM((own, wide), b16),
            pltpu.VMEM((1, wide), f32),
            pltpu.VMEM((1, requests), jnp.int32),
            pltpu.VMEM((1, requests), jnp.int32),
            pltpu.VMEM((3, wide, width), b16),
            pltpu.VMEM((own, width), b16),
            dma((12,)),
            dma((n,)), dma((n,)),
            dma((2,)), dma((2,)),
        ],
        compiler_params=pltpu.CompilerParams(
            collective_id=0, has_side_effects=True, vmem_limit_bytes=VMEM_PROJECT
        ),
        name="project",
    )(
        *map(
            held,
            (
                tokens, first_gain.reshape(1, wide), lengths.reshape(1, requests),
                stream_order.reshape(1, requests), query_weight, key_weight, value_weight,
                cache_keys, cache_values, up_rows,
            ),
        )
    )
    part, new_keys, new_values = pl.pallas_call(
        attend,
        out_shape=(
            shape((n, own, width + HEAD), b16),
            shape((own, width), b16),
            shape((own, width), b16),
        ),
        in_specs=[vmem] * 6,
        out_specs=(vmem,) * 3,
        scratch_shapes=[
            pltpu.VMEM((WIN * heads, rows), f32),
            pltpu.VMEM((WIN * heads, width), f32),
            pltpu.VMEM((requests, width + HEAD), f32),
        ],
        compiler_params=pltpu.CompilerParams(vmem_limit_bytes=VMEM_ATTEND),
        name="attend",
    )(q_all, tab, nk, nv, kb, vb)
    nj = n // nx
    hidden = pl.pallas_call(
        functools.partial(tail, n, t, nx),
        out_shape=shape((own, width), b16),
        in_specs=[free] + [vmem] * 6 + [free, vmem, free],
        out_specs=vmem,
        scratch_shapes=[
            pltpu.VMEM((n, own, width + HEAD), b16),
            pltpu.VMEM((nx, units, wide), b16),
            pltpu.VMEM((nx, units, wide), b16),
            pltpu.VMEM((own, wide), b16),
            pltpu.VMEM((t, own, wide), b16),
            pltpu.VMEM((t, own, width), f32),
            pltpu.VMEM((own, wide), b16),
            pltpu.VMEM((nj, own, wide), b16),
            pltpu.VMEM((nj, t, own, width), b16),
            pltpu.VMEM((nj * t, own, width), b16),
            dma((5,)),
            dma((n,)), dma((n,)),
            dma((2,)), dma((2,)),
            dma((2,)), dma((2,)),
            dma((2,)), dma((2,)),
            dma((t,)), dma((t,)),
            dma((nj,)), dma((nj,)),
            dma((nj * t,)), dma((nj * t,)),
        ],
        compiler_params=pltpu.CompilerParams(
            collective_id=1, has_side_effects=True, vmem_limit_bytes=VMEM_TAIL
        ),
        name="tail",
    )(
        part, q_all, nk, nv, tokens,
        second_gain.reshape(1, wide), out_weight, up_rows, un, down_weight,
    )
    return hidden, new_keys, new_values


def solution(mesh):
    n, t = mesh.shape["req"], mesh.shape["tp"]
    return jax.shard_map(
        functools.partial(body, n, t, 4),
        mesh=mesh,
        in_specs=(
            P("req", None), P(), P(None, "tp"), P(None, "tp"), P(None, "tp"), P("tp", None), P(),
            P(None, ("req", "tp")), P(("req", "tp"), None), P("req", "tp"), P("req", "tp"), P(), P(),
        ),
        out_specs=(P("req", "tp"), P("req", "tp"), P("req", "tp")),
        check_vma=False,
    )
```

```python
import functools

import jax
import jax.numpy as jnp
from jax import lax
from jax.experimental import pallas as pl
from jax.experimental.pallas import tpu as pltpu
from jax.sharding import PartitionSpec as P

HEAD = 128
MESH = pl.DeviceIdType.MESH
NEG = -1e30
WIN = 32
CHUNK = 512
VMEM_PROJECT, VMEM_ATTEND, VMEM_TAIL = 20 << 20, 16 << 20, 16 << 20
NT = (((1,), (1,)), ((), ()))


def norm(v, g):
    center = jnp.mean(v, axis=-1, keepdims=True)
    shifted = v - center
    spread = jnp.mean(shifted * shifted, axis=-1, keepdims=True)
    return shifted * lax.rsqrt(spread + 1e-05) * g


def dot(a, b):
    return jnp.dot(a, b, preferred_element_type=jnp.float32)


def each(lo, hi, f):
    def step(i, carry):
        f(i)
        return carry

    lax.fori_loop(lo, hi, step, 0)


def project(
    n, t, tok_h, gain_h, lens_h, order_h, wq, wk, wv, keys, values, up,
    q_all, nk, nv, tab, kb, vb, un,
    tok, gain, lens, order, wb, qs, wsem, ss, rs, us, ur,
):
    me, z = lax.axis_index("req"), lax.axis_index("tp")
    part = wq.shape[0] // 4
    small = [
        pltpu.make_async_copy(a, b, wsem.at[8 + i])
        for i, (a, b) in enumerate([(tok_h, tok), (gain_h, gain), (lens_h, lens), (order_h, order)])
    ]
    loads = [
        pltpu.make_async_copy(
            wq.at[pl.ds(i * part, part)], wb.at[0, pl.ds(i * part, part)], wsem.at[i]
        )
        for i in range(4)
    ]
    loads += [
        pltpu.make_async_copy(wk, wb.at[1], wsem.at[4]),
        pltpu.make_async_copy(wv, wb.at[2], wsem.at[5]),
        pltpu.make_async_copy(keys, kb, wsem.at[6]),
        pltpu.make_async_copy(values, vb, wsem.at[7]),
    ]
    for load in small + loads[:4]:
        load.start()
    barrier = pltpu.get_barrier_semaphore()

    def greet(d):
        peer = lax.rem(me + d, n)
        pl.semaphore_signal(barrier, inc=1, device_id=(peer, z), device_id_type=MESH)

    each(1, n, greet)
    for d in (1, t - 1):
        pl.semaphore_signal(
            barrier, inc=1, device_id=(me, lax.rem(z + d, t)), device_id_type=MESH
        )
    small[0].wait()
    small[1].wait()
    normed = norm(tok[...].astype(jnp.float32), gain[...]).astype(jnp.bfloat16)
    q = jnp.zeros((tok.shape[0], wq.shape[1]), jnp.float32)
    for i in range(4):
        loads[i].wait()
        q += dot(normed[:, i * part : (i + 1) * part], wb[0, i * part : (i + 1) * part])
    for load in loads[4:]:
        load.start()
    q = (q * HEAD**-0.5).astype(jnp.bfloat16)
    qs[...] = q
    q_all[me] = q
    pl.semaphore_wait(barrier, n + 1)

    def send(d):
        peer = lax.rem(me + d, n)
        pltpu.make_async_remote_copy(
            qs, q_all.at[me], ss.at[d], rs.at[me], device_id=(peer, z), device_id_type=MESH
        ).start()

    each(1, n, send)
    sides = side_copies(up, un, us, ur, me, z, t)
    for copy in sides:
        copy.start()
    loads[4].wait()
    nk[...] = dot(normed, wb[1]).astype(jnp.bfloat16)
    loads[5].wait()
    nv[...] = dot(normed, wb[2]).astype(jnp.bfloat16)
    small[2].wait()
    small[3].wait()
    m = lens.shape[1]
    sub = lax.broadcasted_iota(jnp.int32, (m, m), 0).astype(jnp.float32)
    lane = lax.broadcasted_iota(jnp.int32, (m, m), 1).astype(jnp.float32)
    len_l = lens[...].astype(jnp.float32)
    ord_s = jnp.sum(
        jnp.where(sub == lane, order[...].astype(jnp.float32), 0.0), axis=1, keepdims=True
    )
    hot = ord_s == lane
    rank = jnp.sum(jnp.where(hot, sub, 0.0), axis=0, keepdims=True)
    len_s = jnp.sum(jnp.where(hot, len_l, 0.0), axis=1, keepdims=True)
    end = jnp.sum(jnp.where(sub <= rank, len_s, 0.0), axis=0, keepdims=True)
    tab[0:1] = rank
    tab[1:2] = end - len_l
    tab[2:3] = end
    tab[3:8] = jnp.zeros((5, m), jnp.float32)

    def finish(d):
        src = lax.rem(me + d, n)
        copy = pltpu.make_async_remote_copy(
            qs, q_all.at[src], ss.at[d], rs.at[src], device_id=(src, z), device_id_type=MESH
        )
        copy.wait_recv()
        copy.wait_send()

    each(1, n, finish)
    loads[6].wait()
    loads[7].wait()
    for copy in sides:
        copy.wait()


def side_copies(src, dst, ss, rs, me, z, t):
    return [
        pltpu.make_async_remote_copy(
            src, dst.at[i], ss.at[i], rs.at[i],
            device_id=(me, lax.rem(z + d, t)), device_id_type=MESH,
        )
        for i, d in enumerate((1, t - 1))
    ]


def relay_copies(slots, dst, ss, rs, me, z, t):
    half = dst.shape[0] // 2
    return [
        pltpu.make_async_remote_copy(
            slots.at[i, pl.ds(i * half, half)], dst.at[pl.ds(i * half, half)], ss.at[i], rs.at[i],
            device_id=(me, lax.rem(z + d, t)), device_id_type=MESH,
        )
        for i, d in enumerate((1, t - 1))
    ]


def attend(q_all, tab, nk_in, nv_in, kb, vb, part, nk, nv, sc, acc, put_all):
    rows, width = kb.shape
    heads = width // HEAD
    steps = rows // CHUNK
    nk[...] = nk_in[...]
    nv[...] = nv_in[...]
    base = lax.axis_index("req") * rows
    base_f = base.astype(jnp.float32)
    rank, first, end = tab[0:1], tab[1:2], tab[2:3]
    m = rank.shape[1]
    sub = lax.broadcasted_iota(jnp.int32, (m, m), 0)
    lane = lax.broadcasted_iota(jnp.int32, (m, m), 1)
    diag = sub == lane
    upright = lambda row: jnp.sum(jnp.where(diag, row, 0.0), axis=1, keepdims=True)
    rank_s = upright(rank)
    here = jnp.logical_and(first < base_f + rows, end > base_f)
    here_s = upright(jnp.where(here, 1.0, 0.0)) > 0.5
    low = jnp.min(jnp.where(here, rank, 1e9)).astype(jnp.int32)
    high = jnp.max(jnp.where(here, rank, -1.0)).astype(jnp.int32)
    every_q = q_all[...].astype(jnp.float32).reshape(m, width).astype(jnp.bfloat16)
    tall = WIN * heads
    block = (
        lax.broadcasted_iota(jnp.int32, (tall, width), 0) // WIN
        == lax.broadcasted_iota(jnp.int32, (tall, width), 1) // HEAD
    )
    spot = lax.broadcasted_iota(jnp.int32, (WIN, HEAD), 1)

    def window(slot, opening):
        slot_f = slot.astype(jnp.float32)
        pick = rank == slot_f + lax.broadcasted_iota(jnp.int32, (WIN, m), 0).astype(jnp.float32)
        pick_f = jnp.where(pick, 1.0, 0.0)
        q = dot(pick_f.astype(jnp.bfloat16), every_q)
        first_w = jnp.sum(pick_f * first, axis=1, keepdims=True) - base_f
        end_w = jnp.sum(pick_f * end, axis=1, keepdims=True) - base_f
        first_t = jnp.concatenate([first_w] * heads, axis=0)
        end_t = jnp.concatenate([end_w] * heads, axis=0)
        q_block = jnp.where(block, jnp.concatenate([q] * heads, axis=0), 0.0).astype(jnp.bfloat16)
        top = jnp.full((tall, HEAD), NEG, jnp.float32)
        for i in range(steps):
            s = lax.dot_general(
                q_block, kb[i * CHUNK : (i + 1) * CHUNK], NT, preferred_element_type=jnp.float32
            )
            at = lax.broadcasted_iota(jnp.int32, (tall, CHUNK), 1).astype(jnp.float32) + float(
                i * CHUNK
            )
            s = jnp.where(jnp.logical_and(at >= first_t, at < end_t), s, NEG)
            sc[:, i * CHUNK : (i + 1) * CHUNK] = s
            for j in range(CHUNK // HEAD):
                top = jnp.maximum(top, s[:, j * HEAD : (j + 1) * HEAD])
        peak = jnp.max(top, axis=1, keepdims=True)
        held = jnp.zeros((tall, HEAD), jnp.float32)
        for i in range(steps):
            s = sc[:, i * CHUNK : (i + 1) * CHUNK]
            e = jnp.where(s > 0.1 * NEG, jnp.exp(s - peak), 0.0)
            for j in range(CHUNK // HEAD):
                held += e[:, j * HEAD : (j + 1) * HEAD]
            o = dot(e.astype(jnp.bfloat16), vb[i * CHUNK : (i + 1) * CHUNK])
            if i == 0:
                acc[...] = o
            else:
                acc[...] += o
        mass = jnp.sum(held, axis=1, keepdims=True)
        cut = lambda a, h: a[h * WIN : (h + 1) * WIN]
        stat = jnp.zeros((WIN, HEAD), jnp.float32)
        for h in range(heads):
            stat = jnp.where(spot == h, cut(peak, h), stat)
            stat = jnp.where(spot == heads + h, cut(mass, h), stat)
        found = jnp.concatenate(
            [
                acc[h * WIN : (h + 1) * WIN, h * HEAD : (h + 1) * HEAD] for h in range(heads)
            ]
            + [stat],
            axis=1,
        )
        put = rank_s == slot_f + lax.broadcasted_iota(jnp.int32, (m, WIN), 1).astype(jnp.float32)
        put = jnp.where(put, 1.0, 0.0).astype(jnp.bfloat16)
        one = found.astype(jnp.bfloat16)
        rest = found - one.astype(jnp.float32)
        two = rest.astype(jnp.bfloat16)
        three = (rest - two.astype(jnp.float32)).astype(jnp.bfloat16)
        placed = (dot(put, one) + dot(put, two)) + dot(put, three)
        if opening:
            put_all[...] = placed
        else:
            put_all[...] += placed

    window(low, True)
    each(1, (high - low) // WIN + 1, lambda w: window(low + w * WIN, False))
    stat = put_all[:, width:]
    lanes = lax.broadcasted_iota(jnp.int32, stat.shape, 1)
    stat = jnp.where(jnp.logical_and(lanes < heads, jnp.logical_not(here_s)), NEG, stat)
    one = stat.astype(jnp.bfloat16).astype(jnp.float32)
    two = (stat - one).astype(jnp.bfloat16).astype(jnp.float32)
    three = (stat - one) - two
    kinds = 2 * heads
    stat = jnp.where(
        lanes < kinds,
        one,
        jnp.where(
            lanes < 2 * kinds, pltpu.roll(two, kinds, axis=1), pltpu.roll(three, 2 * kinds, axis=1)
        ),
    )
    shape = part.shape
    part[:, :, :width] = put_all[:, :width].reshape(shape[0], shape[1], width).astype(part.dtype)
    part[:, :, width:] = stat.reshape(shape[0], shape[1], HEAD).astype(part.dtype)


def tail(
    n, t, part, q_all, nk, nv, tok, gain, wo, up, un, down, hid,
    got, upb, dnb, zs, zr, tp, ns, nr, ts, rr, fs, fr,
    lsem, a_s, a_r, u_s, u_r, d_s, d_r, e_s, e_r, z_s, z_r, n_s, n_r, r_s, r_r, f_s, f_r,
):
    me, z = lax.axis_index("req"), lax.axis_index("tp")
    f32, b16 = jnp.float32, jnp.bfloat16
    width = q_all.shape[2]
    heads = width // HEAD
    own, wide = tok.shape
    few = own // t
    loads = [
        pltpu.make_async_copy(up, upb.at[0], lsem.at[0]),
        pltpu.make_async_copy(down, dnb.at[0], lsem.at[1]),
        pltpu.make_async_copy(part.at[me], got.at[me], lsem.at[2]),
        pltpu.make_async_copy(un, upb.at[pl.ds(1, 2)], lsem.at[3]),
    ]
    for load in loads:
        load.start()
    barrier = pltpu.get_barrier_semaphore()

    def greet(d):
        peer = lax.rem(me + d, n)
        pl.semaphore_signal(barrier, inc=1, device_id=(peer, z), device_id_type=MESH)

    each(1, n, greet)

    def greet_z(d):
        pl.semaphore_signal(
            barrier, inc=1, device_id=(me, lax.rem(z + d, t)), device_id_type=MESH
        )

    each(1, t, greet_z)
    pl.semaphore_wait(barrier, n - 1 + t - 1)

    def line_copies(src, dst, ss, rs):
        def one(d, s, peer):
            return pltpu.make_async_remote_copy(
                src(peer), dst.at[s], ss.at[d], rs.at[s], device_id=(peer, z), device_id_type=MESH
            )

        def start():
            each(1, n, lambda d: one(d, me, lax.rem(me + d, n)).start())

        def finish():
            def wait(d):
                other = lax.rem(me + d, n)
                copy = one(d, other, other)
                copy.wait_recv()
                copy.wait_send()

            each(1, n, wait)

        return start, finish

    def z_copies(src, dst, ss, rs):
        def one(d, s):
            peer = lax.rem(z + d, t)
            return pltpu.make_async_remote_copy(
                src(peer), dst.at[s], ss.at[d], rs.at[s], device_id=(me, peer), device_id_type=MESH
            )

        def start():
            each(1, t, lambda d: one(d, z).start())

        def finish():
            def wait(d):
                copy = one(d, lax.rem(z + d, t))
                copy.wait_recv()
                copy.wait_send()

            each(1, t, wait)

        return start, finish

    send, take = line_copies(lambda peer: part.at[peer], got, a_s, a_r)
    send()
    sides = dnb.at[pl.ds(1, 2)]
    up_relay = relay_copies(un, upb.at[t - 1], u_s, u_r, me, z, t)
    down_side = side_copies(down, sides, d_s, d_r, me, z, t)
    down_relay = relay_copies(sides, dnb.at[t - 1], e_s, e_r, me, z, t)
    for copy in up_relay + down_side:
        copy.start()

    def pieces(a):
        return [
            jnp.concatenate(
                [a[k * few : (k + 1) * few, b * width : (b + 1) * width] for b in range(t)], axis=0
            )
            for k in range(t)
        ]

    q = q_all[me].astype(f32)
    kn = nk[...].astype(f32)
    vn = nv[...].astype(f32)
    spot = lax.broadcasted_iota(jnp.int32, (own, HEAD), 1)
    mine = jnp.zeros((own, HEAD), f32)
    for h in range(heads):
        cols = slice(h * HEAD, (h + 1) * HEAD)
        mine = jnp.where(spot == h, jnp.sum(q[:, cols] * kn[:, cols], axis=1, keepdims=True), mine)
    for k, piece in enumerate(pieces(tok[...].astype(f32))):
        tp[k] = piece
    gains = jnp.concatenate(
        [
            jnp.broadcast_to(gain[:, b * width : (b + 1) * width], (few, width)) for b in range(t)
        ],
        axis=0,
    )
    loads[2].wait()
    take()
    kinds = 2 * heads
    coded = got[:, :, width:].astype(f32)
    stat = (coded + pltpu.roll(coded, HEAD - kinds, axis=2)) + pltpu.roll(
        coded, HEAD - 2 * kinds, axis=2
    )
    top = jnp.maximum(jnp.max(stat, axis=0), mine)
    scale = jnp.exp(stat - top[None])
    mass = pltpu.roll(stat, HEAD - heads, axis=2)
    self_w = jnp.exp(mine - top)
    total = self_w + jnp.sum(scale * mass, axis=0)
    attended = []
    for h in range(heads):
        cols = slice(h * HEAD, (h + 1) * HEAD)
        older = jnp.sum(got[:, :, cols].astype(f32) * scale[:, :, h : h + 1], axis=0)
        attended.append((self_w[:, h : h + 1] * vn[:, cols] + older) / total[:, h : h + 1])
    attended = jnp.concatenate(attended, axis=1).astype(b16)
    for k, piece in enumerate(pieces(dot(attended, wo[...]))):
        zs[k] = piece
    send, take = z_copies(lambda peer: zs.at[peer], zr, z_s, z_r)
    send()
    mid = zs[z]
    take()
    for i in range(1, t):
        mid += zr[lax.rem(z + i, t)]
    mid += tp[z]
    for copy in down_side:
        copy.wait()
    for copy in down_relay:
        copy.start()

    def mean(a):
        r = jnp.broadcast_to(jnp.sum(a, axis=1, keepdims=True), (own, HEAD))
        whole = r
        for b in range(1, t):
            whole += pltpu.roll(r, b * few, axis=0)
        return whole[:, :1] / wide

    shifted = mid - mean(mid)
    normed = (shifted * lax.rsqrt(mean(shifted * shifted) + 1e-05) * gains).astype(b16)
    ns[...] = normed
    nr[me] = normed
    send, take = line_copies(lambda peer: ns, nr, n_s, n_r)
    send()
    loads[0].wait()
    loads[3].wait()
    for copy in up_relay:
        copy.wait()
    take()
    rows, units = n * own, t * up.shape[0]
    row_block = lax.rem(lax.broadcasted_iota(jnp.int32, (rows, width), 0), own) // few
    x = nr[...].astype(f32).reshape(rows, width).astype(b16)
    pre = jnp.zeros((rows, units), f32)
    for b in range(t):
        y = lax.dot_general(
            x, upb[:, :, b * width : (b + 1) * width].reshape(units, width), NT,
            preferred_element_type=f32,
        )
        pre = jnp.where(row_block[:, :units] == b, y, pre)
    pre = pre.reshape(n, own, units)
    whole = pre
    for b in range(1, t):
        whole += pltpu.roll(pre, b * few, axis=1)
    act = (0.5 * whole * (1.0 + lax.erf(whole * 0.5**0.5))).reshape(rows, units).astype(b16)
    loads[1].wait()
    for copy in down_relay:
        copy.wait()
    term = jnp.zeros((rows, width), f32)
    for b in range(t):
        y = dot(act, dnb[:, :, b * width : (b + 1) * width].reshape(units, width))
        term = jnp.where(row_block == b, y, term)
    term = term.reshape(n, own, width).astype(b16)
    ts[...] = term
    send, take = line_copies(lambda peer: ts.at[peer], rr, r_s, r_r)
    send()
    rr[me] = ts[me]
    take()
    out = (mid + jnp.sum(rr[...].astype(f32), axis=0)).astype(b16)
    fs[...] = out
    fr[z] = out
    send, take = z_copies(lambda peer: fs, fr, f_s, f_r)
    send()
    take()
    every = [fr[k].astype(f32) for k in range(t)]
    final = jnp.zeros((own, width), f32)
    for b in range(t):
        rows_b = jnp.concatenate([a[b * few : (b + 1) * few] for a in every], axis=0)
        final = jnp.where(z == b, rows_b, final)
    hid[...] = final.astype(b16)


def body(
    n, t, tokens, first_gain, query_weight, key_weight, value_weight, out_weight, second_gain,
    up_weight, down_weight, cache_keys, cache_values, lengths, stream_order,
):
    f32, b16 = jnp.float32, jnp.bfloat16
    own, wide = tokens.shape
    width = query_weight.shape[1]
    requests = own * n
    units = up_weight.shape[1]
    rows = cache_keys.shape[0]
    steps = rows // CHUNK
    vmem = pl.BlockSpec(memory_space=pltpu.VMEM)
    hbm = pl.BlockSpec(memory_space=pltpu.HBM)
    free = pl.BlockSpec(memory_space=pl.ANY)
    dma = pltpu.SemaphoreType.DMA
    shape = jax.ShapeDtypeStruct
    up_rows = up_weight.T
    held = lambda a: pltpu.with_memory_space_constraint(a, pltpu.HBM)
    heads = width // HEAD
    q_all, nk, nv, tab, kb, vb, un = pl.pallas_call(
        functools.partial(project, n, t),
        out_shape=(
            shape((n, own, width), b16),
            shape((own, width), b16),
            shape((own, width), b16),
            shape((8, requests), f32),
            shape((rows, width), b16),
            shape((rows, width), b16),
            shape((2, units, wide), b16),
        ),
        in_specs=[hbm] * 10,
        out_specs=(vmem,) * 7,
        scratch_shapes=[
            pltpu.VMEM((own, wide), b16),
            pltpu.VMEM((1, wide), f32),
            pltpu.VMEM((1, requests), jnp.int32),
            pltpu.VMEM((1, requests), jnp.int32),
            pltpu.VMEM((3, wide, width), b16),
            pltpu.VMEM((own, width), b16),
            dma((12,)),
            dma((n,)), dma((n,)),
            dma((2,)), dma((2,)),
        ],
        compiler_params=pltpu.CompilerParams(
            collective_id=0, has_side_effects=True, vmem_limit_bytes=VMEM_PROJECT
        ),
        name="project",
    )(
        *map(
            held,
            (
                tokens, first_gain.reshape(1, wide), lengths.reshape(1, requests),
                stream_order.reshape(1, requests), query_weight, key_weight, value_weight,
                cache_keys, cache_values, up_rows,
            ),
        )
    )
    part, new_keys, new_values = pl.pallas_call(
        attend,
        out_shape=(
            shape((n, own, width + HEAD), b16),
            shape((own, width), b16),
            shape((own, width), b16),
        ),
        in_specs=[vmem] * 6,
        out_specs=(vmem,) * 3,
        scratch_shapes=[
            pltpu.VMEM((WIN * heads, rows), f32),
            pltpu.VMEM((WIN * heads, width), f32),
            pltpu.VMEM((requests, width + HEAD), f32),
        ],
        compiler_params=pltpu.CompilerParams(vmem_limit_bytes=VMEM_ATTEND),
        name="attend",
    )(q_all, tab, nk, nv, kb, vb)
    hidden = pl.pallas_call(
        functools.partial(tail, n, t),
        out_shape=shape((own, width), b16),
        in_specs=[free] + [vmem] * 6 + [free, vmem, free],
        out_specs=vmem,
        scratch_shapes=[
            pltpu.VMEM((n, own, width + HEAD), b16),
            pltpu.VMEM((t, units, wide), b16),
            pltpu.VMEM((t, units, wide), b16),
            pltpu.VMEM((t, own, width), f32),
            pltpu.VMEM((t, own, width), f32),
            pltpu.VMEM((t, own, width), f32),
            pltpu.VMEM((own, width), b16),
            pltpu.VMEM((n, own, width), b16),
            pltpu.VMEM((n, own, width), b16),
            pltpu.VMEM((n, own, width), b16),
            pltpu.VMEM((own, width), b16),
            pltpu.VMEM((t, own, width), b16),
            dma((4,)),
            dma((n,)), dma((n,)),
            dma((2,)), dma((2,)),
            dma((2,)), dma((2,)),
            dma((2,)), dma((2,)),
            dma((t,)), dma((t,)),
            dma((n,)), dma((n,)),
            dma((n,)), dma((n,)),
            dma((t,)), dma((t,)),
        ],
        compiler_params=pltpu.CompilerParams(
            collective_id=1, has_side_effects=True, vmem_limit_bytes=VMEM_TAIL
        ),
        name="tail",
    )(
        part, q_all, nk, nv, tokens,
        second_gain.reshape(1, wide), out_weight, up_rows, un, down_weight,
    )
    return hidden, new_keys, new_values


def solution(mesh):
    n, t = mesh.shape["req"], mesh.shape["tp"]
    return jax.shard_map(
        functools.partial(body, n, t),
        mesh=mesh,
        in_specs=(
            P("req", None), P(), P(None, "tp"), P(None, "tp"), P(None, "tp"), P("tp", None), P(),
            P(None, ("req", "tp")), P(("req", "tp"), None), P("req", "tp"), P("req", "tp"), P(), P(),
        ),
        out_specs=(P("req", "tp"), P("req", "tp"), P("req", "tp")),
        check_vma=False,
    )
```

```python
import functools
import math

import jax
import jax.numpy as jnp
from jax import lax
from jax.experimental import pallas as pl
from jax.experimental.pallas import tpu as pltpu
from jax.sharding import PartitionSpec as P

HEAD = 128
MESH = pl.DeviceIdType.MESH
NEG = -1e30
WIN = 32
CHUNK = 512
VMEM_PROJECT, VMEM_ATTEND, VMEM_TAIL = 20 << 20, 16 << 20, 16 << 20
NT = (((1,), (1,)), ((), ()))


def norm(v, g):
    center = jnp.mean(v, axis=-1, keepdims=True)
    shifted = v - center
    spread = jnp.mean(shifted * shifted, axis=-1, keepdims=True)
    return shifted * lax.rsqrt(spread + 1e-05) * g


def dot(a, b):
    return jnp.dot(a, b, preferred_element_type=jnp.float32)


def each(lo, hi, f):
    def step(i, carry):
        f(i)
        return carry

    lax.fori_loop(lo, hi, step, 0)


def line(n, me):
    side = math.isqrt(n // 2)
    y, x, c = me // (2 * side), lax.rem(me // 2, side), lax.rem(me, 2)
    far = lambda o: min(o[0], side - o[0]) + min(o[1], side - o[1])
    steps = [(i, j, k) for i in range(side) for j in range(side) for k in range(2)]
    steps = sorted(steps[1:], key=lambda o: (-far(o), -o[2]))
    ys = [lax.rem(y + i, side) for i in range(side)]
    xs = [lax.rem(x + i, side) for i in range(side)]
    cs = [c, 1 - c]
    return [(i, (ys[a] * side + xs[b]) * 2 + cs[k]) for i, (a, b, k) in enumerate(steps)]


def ring(t, z):
    steps = sorted(range(1, t), key=lambda d: -min(d, t - d))
    return [(d, lax.rem(z + d, t)) for d in steps]


def project(
    n, t, tok_h, gain_h, lens_h, order_h, wq, wk, wv, keys, values, up,
    q_all, nk, nv, tab, kb, vb, un,
    tok, gain, lens, order, wb, qs, wsem, ss, rs, us, ur,
):
    me, z = lax.axis_index("req"), lax.axis_index("tp")
    part = wq.shape[0] // 4
    small = [
        pltpu.make_async_copy(a, b, wsem.at[8 + i])
        for i, (a, b) in enumerate([(tok_h, tok), (gain_h, gain), (lens_h, lens), (order_h, order)])
    ]
    loads = [
        pltpu.make_async_copy(
            wq.at[pl.ds(i * part, part)], wb.at[0, pl.ds(i * part, part)], wsem.at[i]
        )
        for i in range(4)
    ]
    loads += [
        pltpu.make_async_copy(wk, wb.at[1], wsem.at[4]),
        pltpu.make_async_copy(wv, wb.at[2], wsem.at[5]),
        pltpu.make_async_copy(keys, kb, wsem.at[6]),
        pltpu.make_async_copy(values, vb, wsem.at[7]),
    ]
    for load in small + loads[:4]:
        load.start()
    barrier = pltpu.get_barrier_semaphore()

    others = line(n, me)
    for _, peer in others:
        pl.semaphore_signal(barrier, inc=1, device_id=(peer, z), device_id_type=MESH)
    for d in (1, t - 1):
        pl.semaphore_signal(
            barrier, inc=1, device_id=(me, lax.rem(z + d, t)), device_id_type=MESH
        )
    small[0].wait()
    small[1].wait()
    normed = norm(tok[...].astype(jnp.float32), gain[...]).astype(jnp.bfloat16)
    pl.semaphore_wait(barrier, n + 1)
    sides = side_copies(up, un, us, ur, me, z, t)
    for copy in sides:
        copy.start()
    q = jnp.zeros((tok.shape[0], wq.shape[1]), jnp.float32)
    for i in range(4):
        loads[i].wait()
        q += dot(normed[:, i * part : (i + 1) * part], wb[0, i * part : (i + 1) * part])
    for load in loads[4:]:
        load.start()
    q = (q * HEAD**-0.5).astype(jnp.bfloat16)
    qs[...] = q
    q_all[me] = q
    for i, peer in others:
        pltpu.make_async_remote_copy(
            qs, q_all.at[me], ss.at[i], rs.at[me], device_id=(peer, z), device_id_type=MESH
        ).start()
    loads[4].wait()
    nk[...] = dot(normed, wb[1]).astype(jnp.bfloat16)
    loads[5].wait()
    nv[...] = dot(normed, wb[2]).astype(jnp.bfloat16)
    small[2].wait()
    small[3].wait()
    m = lens.shape[1]
    sub = lax.broadcasted_iota(jnp.int32, (m, m), 0).astype(jnp.float32)
    lane = lax.broadcasted_iota(jnp.int32, (m, m), 1).astype(jnp.float32)
    len_l = lens[...].astype(jnp.float32)
    ord_s = jnp.sum(
        jnp.where(sub == lane, order[...].astype(jnp.float32), 0.0), axis=1, keepdims=True
    )
    hot = ord_s == lane
    rank = jnp.sum(jnp.where(hot, sub, 0.0), axis=0, keepdims=True)
    len_s = jnp.sum(jnp.where(hot, len_l, 0.0), axis=1, keepdims=True)
    end = jnp.sum(jnp.where(sub <= rank, len_s, 0.0), axis=0, keepdims=True)
    tab[0:1] = rank
    tab[1:2] = end - len_l
    tab[2:3] = end
    tab[3:8] = jnp.zeros((5, m), jnp.float32)

    for i, src in others:
        copy = pltpu.make_async_remote_copy(
            qs, q_all.at[src], ss.at[i], rs.at[src], device_id=(src, z), device_id_type=MESH
        )
        copy.wait_recv()
        copy.wait_send()
    loads[6].wait()
    loads[7].wait()
    for copy in sides:
        copy.wait()


def side_copies(src, dst, ss, rs, me, z, t):
    return [
        pltpu.make_async_remote_copy(
            src, dst.at[i], ss.at[i], rs.at[i],
            device_id=(me, lax.rem(z + d, t)), device_id_type=MESH,
        )
        for i, d in enumerate((1, t - 1))
    ]


def relay_copies(slots, dst, ss, rs, me, z, t):
    half = dst.shape[0] // 2
    return [
        pltpu.make_async_remote_copy(
            slots.at[i, pl.ds(i * half, half)], dst.at[pl.ds(i * half, half)], ss.at[i], rs.at[i],
            device_id=(me, lax.rem(z + d, t)), device_id_type=MESH,
        )
        for i, d in enumerate((1, t - 1))
    ]


def attend(q_all, tab, nk_in, nv_in, kb, vb, part, nk, nv, sc, acc, put_all):
    rows, width = kb.shape
    heads = width // HEAD
    steps = rows // CHUNK
    nk[...] = nk_in[...]
    nv[...] = nv_in[...]
    base = lax.axis_index("req") * rows
    base_f = base.astype(jnp.float32)
    rank, first, end = tab[0:1], tab[1:2], tab[2:3]
    m = rank.shape[1]
    sub = lax.broadcasted_iota(jnp.int32, (m, m), 0)
    lane = lax.broadcasted_iota(jnp.int32, (m, m), 1)
    diag = sub == lane
    upright = lambda row: jnp.sum(jnp.where(diag, row, 0.0), axis=1, keepdims=True)
    rank_s = upright(rank)
    here = jnp.logical_and(first < base_f + rows, end > base_f)
    here_s = upright(jnp.where(here, 1.0, 0.0)) > 0.5
    low = jnp.min(jnp.where(here, rank, 1e9)).astype(jnp.int32)
    high = jnp.max(jnp.where(here, rank, -1.0)).astype(jnp.int32)
    every_q = q_all[...].astype(jnp.float32).reshape(m, width).astype(jnp.bfloat16)
    tall = WIN * heads
    block = (
        lax.broadcasted_iota(jnp.int32, (tall, width), 0) // WIN
        == lax.broadcasted_iota(jnp.int32, (tall, width), 1) // HEAD
    )
    spot = lax.broadcasted_iota(jnp.int32, (WIN, HEAD), 1)

    def window(slot, opening):
        slot_f = slot.astype(jnp.float32)
        pick = rank == slot_f + lax.broadcasted_iota(jnp.int32, (WIN, m), 0).astype(jnp.float32)
        pick_f = jnp.where(pick, 1.0, 0.0)
        q = dot(pick_f.astype(jnp.bfloat16), every_q)
        first_w = jnp.sum(pick_f * first, axis=1, keepdims=True) - base_f
        end_w = jnp.sum(pick_f * end, axis=1, keepdims=True) - base_f
        first_t = jnp.concatenate([first_w] * heads, axis=0)
        end_t = jnp.concatenate([end_w] * heads, axis=0)
        q_block = jnp.where(block, jnp.concatenate([q] * heads, axis=0), 0.0).astype(jnp.bfloat16)
        top = jnp.full((tall, HEAD), NEG, jnp.float32)
        for i in range(steps):
            s = lax.dot_general(
                q_block, kb[i * CHUNK : (i + 1) * CHUNK], NT, preferred_element_type=jnp.float32
            )
            at = lax.broadcasted_iota(jnp.int32, (tall, CHUNK), 1).astype(jnp.float32) + float(
                i * CHUNK
            )
            s = jnp.where(jnp.logical_and(at >= first_t, at < end_t), s, NEG)
            sc[:, i * CHUNK : (i + 1) * CHUNK] = s
            for j in range(CHUNK // HEAD):
                top = jnp.maximum(top, s[:, j * HEAD : (j + 1) * HEAD])
        peak = jnp.max(top, axis=1, keepdims=True)
        held = jnp.zeros((tall, HEAD), jnp.float32)
        for i in range(steps):
            s = sc[:, i * CHUNK : (i + 1) * CHUNK]
            e = jnp.where(s > 0.1 * NEG, jnp.exp(s - peak), 0.0)
            for j in range(CHUNK // HEAD):
                held += e[:, j * HEAD : (j + 1) * HEAD]
            o = dot(e.astype(jnp.bfloat16), vb[i * CHUNK : (i + 1) * CHUNK])
            if i == 0:
                acc[...] = o
            else:
                acc[...] += o
        mass = jnp.sum(held, axis=1, keepdims=True)
        cut = lambda a, h: a[h * WIN : (h + 1) * WIN]
        stat = jnp.zeros((WIN, HEAD), jnp.float32)
        for h in range(heads):
            stat = jnp.where(spot == h, cut(peak, h), stat)
            stat = jnp.where(spot == heads + h, cut(mass, h), stat)
        found = jnp.concatenate(
            [
                acc[h * WIN : (h + 1) * WIN, h * HEAD : (h + 1) * HEAD] for h in range(heads)
            ]
            + [stat],
            axis=1,
        )
        put = rank_s == slot_f + lax.broadcasted_iota(jnp.int32, (m, WIN), 1).astype(jnp.float32)
        put = jnp.where(put, 1.0, 0.0).astype(jnp.bfloat16)
        one = found.astype(jnp.bfloat16)
        rest = found - one.astype(jnp.float32)
        two = rest.astype(jnp.bfloat16)
        three = (rest - two.astype(jnp.float32)).astype(jnp.bfloat16)
        placed = (dot(put, one) + dot(put, two)) + dot(put, three)
        if opening:
            put_all[...] = placed
        else:
            put_all[...] += placed

    window(low, True)
    each(1, (high - low) // WIN + 1, lambda w: window(low + w * WIN, False))
    stat = put_all[:, width:]
    lanes = lax.broadcasted_iota(jnp.int32, stat.shape, 1)
    stat = jnp.where(jnp.logical_and(lanes < heads, jnp.logical_not(here_s)), NEG, stat)
    one = stat.astype(jnp.bfloat16).astype(jnp.float32)
    two = (stat - one).astype(jnp.bfloat16).astype(jnp.float32)
    three = (stat - one) - two
    kinds = 2 * heads
    stat = jnp.where(
        lanes < kinds,
        one,
        jnp.where(
            lanes < 2 * kinds, pltpu.roll(two, kinds, axis=1), pltpu.roll(three, 2 * kinds, axis=1)
        ),
    )
    shape = part.shape
    part[:, :, :width] = put_all[:, :width].reshape(shape[0], shape[1], width).astype(part.dtype)
    part[:, :, width:] = stat.reshape(shape[0], shape[1], HEAD).astype(part.dtype)


def tail(
    n, t, part, q_all, nk, nv, tok, gain, wo, up, un, down, hid,
    got, upb, dnb, zs, zr, tp, ns, nr, ts, rr, fs, fr,
    lsem, a_s, a_r, u_s, u_r, d_s, d_r, e_s, e_r, z_s, z_r, n_s, n_r, r_s, r_r, f_s, f_r,
):
    me, z = lax.axis_index("req"), lax.axis_index("tp")
    f32, b16 = jnp.float32, jnp.bfloat16
    width = q_all.shape[2]
    heads = width // HEAD
    own, wide = tok.shape
    few = own // t
    loads = [
        pltpu.make_async_copy(up, upb.at[0], lsem.at[0]),
        pltpu.make_async_copy(down, dnb.at[0], lsem.at[1]),
        pltpu.make_async_copy(part.at[me], got.at[me], lsem.at[2]),
        pltpu.make_async_copy(un, upb.at[pl.ds(1, 2)], lsem.at[3]),
    ]
    for load in loads:
        load.start()
    barrier = pltpu.get_barrier_semaphore()

    others, others_z = line(n, me), ring(t, z)
    for _, peer in others:
        pl.semaphore_signal(barrier, inc=1, device_id=(peer, z), device_id_type=MESH)
    for _, peer in others_z:
        pl.semaphore_signal(barrier, inc=1, device_id=(me, peer), device_id_type=MESH)
    pl.semaphore_wait(barrier, n - 1 + t - 1)

    def line_copies(src, dst, ss, rs):
        def one(d, s, peer):
            return pltpu.make_async_remote_copy(
                src(peer), dst.at[s], ss.at[d], rs.at[s], device_id=(peer, z), device_id_type=MESH
            )

        def start():
            for i, peer in others:
                one(i, me, peer).start()

        def finish():
            for i, peer in others:
                copy = one(i, peer, peer)
                copy.wait_recv()
                copy.wait_send()

        return start, finish

    def z_copies(src, dst, ss, rs):
        def one(d, s, peer):
            return pltpu.make_async_remote_copy(
                src(peer), dst.at[s], ss.at[d], rs.at[s], device_id=(me, peer), device_id_type=MESH
            )

        def start():
            for d, peer in others_z:
                one(d, z, peer).start()

        def finish():
            for d, peer in others_z:
                copy = one(d, peer, peer)
                copy.wait_recv()
                copy.wait_send()

        return start, finish

    send, take = line_copies(lambda peer: part.at[peer], got, a_s, a_r)
    send()
    sides = dnb.at[pl.ds(1, 2)]
    up_relay = relay_copies(un, upb.at[t - 1], u_s, u_r, me, z, t)
    down_side = side_copies(down, sides, d_s, d_r, me, z, t)
    down_relay = relay_copies(sides, dnb.at[t - 1], e_s, e_r, me, z, t)
    for copy in up_relay + down_side:
        copy.start()

    def pieces(a):
        return [
            jnp.concatenate(
                [a[k * few : (k + 1) * few, b * width : (b + 1) * width] for b in range(t)], axis=0
            )
            for k in range(t)
        ]

    q = q_all[me].astype(f32)
    kn = nk[...].astype(f32)
    vn = nv[...].astype(f32)
    spot = lax.broadcasted_iota(jnp.int32, (own, HEAD), 1)
    mine = jnp.zeros((own, HEAD), f32)
    for h in range(heads):
        cols = slice(h * HEAD, (h + 1) * HEAD)
        mine = jnp.where(spot == h, jnp.sum(q[:, cols] * kn[:, cols], axis=1, keepdims=True), mine)
    for k, piece in enumerate(pieces(tok[...].astype(f32))):
        tp[k] = piece
    gains = jnp.concatenate(
        [
            jnp.broadcast_to(gain[:, b * width : (b + 1) * width], (few, width)) for b in range(t)
        ],
        axis=0,
    )
    loads[2].wait()
    take()
    kinds = 2 * heads
    coded = got[:, :, width:].astype(f32)
    stat = (coded + pltpu.roll(coded, HEAD - kinds, axis=2)) + pltpu.roll(
        coded, HEAD - 2 * kinds, axis=2
    )
    top = jnp.maximum(jnp.max(stat, axis=0), mine)
    scale = jnp.exp(stat - top[None])
    mass = pltpu.roll(stat, HEAD - heads, axis=2)
    self_w = jnp.exp(mine - top)
    total = self_w + jnp.sum(scale * mass, axis=0)
    attended = []
    for h in range(heads):
        cols = slice(h * HEAD, (h + 1) * HEAD)
        older = jnp.sum(got[:, :, cols].astype(f32) * scale[:, :, h : h + 1], axis=0)
        attended.append((self_w[:, h : h + 1] * vn[:, cols] + older) / total[:, h : h + 1])
    attended = jnp.concatenate(attended, axis=1).astype(b16)
    for k, piece in enumerate(pieces(dot(attended, wo[...]))):
        zs[k] = piece
    send, take = z_copies(lambda peer: zs.at[peer], zr, z_s, z_r)
    send()
    mid = zs[z]
    take()
    for i in range(1, t):
        mid += zr[lax.rem(z + i, t)]
    mid += tp[z]
    for copy in down_side:
        copy.wait()
    for copy in down_relay:
        copy.start()

    def mean(a):
        r = jnp.broadcast_to(jnp.sum(a, axis=1, keepdims=True), (own, HEAD))
        whole = r
        for b in range(1, t):
            whole += pltpu.roll(r, b * few, axis=0)
        return whole[:, :1] / wide

    shifted = mid - mean(mid)
    normed = (shifted * lax.rsqrt(mean(shifted * shifted) + 1e-05) * gains).astype(b16)
    ns[...] = normed
    nr[me] = normed
    send, take = line_copies(lambda peer: ns, nr, n_s, n_r)
    send()
    loads[0].wait()
    loads[3].wait()
    for copy in up_relay:
        copy.wait()
    take()
    rows, units = n * own, t * up.shape[0]
    row_block = lax.rem(lax.broadcasted_iota(jnp.int32, (rows, width), 0), own) // few
    x = nr[...].astype(f32).reshape(rows, width).astype(b16)
    pre = jnp.zeros((rows, units), f32)
    for b in range(t):
        y = lax.dot_general(
            x, upb[:, :, b * width : (b + 1) * width].reshape(units, width), NT,
            preferred_element_type=f32,
        )
        pre = jnp.where(row_block[:, :units] == b, y, pre)
    pre = pre.reshape(n, own, units)
    whole = pre
    for b in range(1, t):
        whole += pltpu.roll(pre, b * few, axis=1)
    act = (0.5 * whole * (1.0 + lax.erf(whole * 0.5**0.5))).reshape(rows, units).astype(b16)
    loads[1].wait()
    for copy in down_relay:
        copy.wait()
    term = jnp.zeros((rows, width), f32)
    for b in range(t):
        y = dot(act, dnb[:, :, b * width : (b + 1) * width].reshape(units, width))
        term = jnp.where(row_block == b, y, term)
    term = term.reshape(n, own, width).astype(b16)
    ts[...] = term
    send, take = line_copies(lambda peer: ts.at[peer], rr, r_s, r_r)
    send()
    rr[me] = ts[me]
    take()
    out = (mid + jnp.sum(rr[...].astype(f32), axis=0)).astype(b16)
    fs[...] = out
    fr[z] = out
    send, take = z_copies(lambda peer: fs, fr, f_s, f_r)
    send()
    take()
    every = [fr[k].astype(f32) for k in range(t)]
    final = jnp.zeros((own, width), f32)
    for b in range(t):
        rows_b = jnp.concatenate([a[b * few : (b + 1) * few] for a in every], axis=0)
        final = jnp.where(z == b, rows_b, final)
    hid[...] = final.astype(b16)


def body(
    n, t, tokens, first_gain, query_weight, key_weight, value_weight, out_weight, second_gain,
    up_weight, down_weight, cache_keys, cache_values, lengths, stream_order,
):
    f32, b16 = jnp.float32, jnp.bfloat16
    own, wide = tokens.shape
    width = query_weight.shape[1]
    requests = own * n
    units = up_weight.shape[1]
    rows = cache_keys.shape[0]
    steps = rows // CHUNK
    vmem = pl.BlockSpec(memory_space=pltpu.VMEM)
    hbm = pl.BlockSpec(memory_space=pltpu.HBM)
    free = pl.BlockSpec(memory_space=pl.ANY)
    dma = pltpu.SemaphoreType.DMA
    shape = jax.ShapeDtypeStruct
    up_rows = up_weight.T
    held = lambda a: pltpu.with_memory_space_constraint(a, pltpu.HBM)
    heads = width // HEAD
    q_all, nk, nv, tab, kb, vb, un = pl.pallas_call(
        functools.partial(project, n, t),
        out_shape=(
            shape((n, own, width), b16),
            shape((own, width), b16),
            shape((own, width), b16),
            shape((8, requests), f32),
            shape((rows, width), b16),
            shape((rows, width), b16),
            shape((2, units, wide), b16),
        ),
        in_specs=[hbm] * 10,
        out_specs=(vmem,) * 7,
        scratch_shapes=[
            pltpu.VMEM((own, wide), b16),
            pltpu.VMEM((1, wide), f32),
            pltpu.VMEM((1, requests), jnp.int32),
            pltpu.VMEM((1, requests), jnp.int32),
            pltpu.VMEM((3, wide, width), b16),
            pltpu.VMEM((own, width), b16),
            dma((12,)),
            dma((n,)), dma((n,)),
            dma((2,)), dma((2,)),
        ],
        compiler_params=pltpu.CompilerParams(
            collective_id=0, has_side_effects=True, vmem_limit_bytes=VMEM_PROJECT
        ),
        name="project",
    )(
        *map(
            held,
            (
                tokens, first_gain.reshape(1, wide), lengths.reshape(1, requests),
                stream_order.reshape(1, requests), query_weight, key_weight, value_weight,
                cache_keys, cache_values, up_rows,
            ),
        )
    )
    part, new_keys, new_values = pl.pallas_call(
        attend,
        out_shape=(
            shape((n, own, width + HEAD), b16),
            shape((own, width), b16),
            shape((own, width), b16),
        ),
        in_specs=[vmem] * 6,
        out_specs=(vmem,) * 3,
        scratch_shapes=[
            pltpu.VMEM((WIN * heads, rows), f32),
            pltpu.VMEM((WIN * heads, width), f32),
            pltpu.VMEM((requests, width + HEAD), f32),
        ],
        compiler_params=pltpu.CompilerParams(vmem_limit_bytes=VMEM_ATTEND),
        name="attend",
    )(q_all, tab, nk, nv, kb, vb)
    hidden = pl.pallas_call(
        functools.partial(tail, n, t),
        out_shape=shape((own, width), b16),
        in_specs=[free] + [vmem] * 6 + [free, vmem, free],
        out_specs=vmem,
        scratch_shapes=[
            pltpu.VMEM((n, own, width + HEAD), b16),
            pltpu.VMEM((t, units, wide), b16),
            pltpu.VMEM((t, units, wide), b16),
            pltpu.VMEM((t, own, width), f32),
            pltpu.VMEM((t, own, width), f32),
            pltpu.VMEM((t, own, width), f32),
            pltpu.VMEM((own, width), b16),
            pltpu.VMEM((n, own, width), b16),
            pltpu.VMEM((n, own, width), b16),
            pltpu.VMEM((n, own, width), b16),
            pltpu.VMEM((own, width), b16),
            pltpu.VMEM((t, own, width), b16),
            dma((4,)),
            dma((n,)), dma((n,)),
            dma((2,)), dma((2,)),
            dma((2,)), dma((2,)),
            dma((2,)), dma((2,)),
            dma((t,)), dma((t,)),
            dma((n,)), dma((n,)),
            dma((n,)), dma((n,)),
            dma((t,)), dma((t,)),
        ],
        compiler_params=pltpu.CompilerParams(
            collective_id=1, has_side_effects=True, vmem_limit_bytes=VMEM_TAIL
        ),
        name="tail",
    )(
        part, q_all, nk, nv, tokens,
        second_gain.reshape(1, wide), out_weight, up_rows, un, down_weight,
    )
    return hidden, new_keys, new_values


def solution(mesh):
    n, t = mesh.shape["req"], mesh.shape["tp"]
    return jax.shard_map(
        functools.partial(body, n, t),
        mesh=mesh,
        in_specs=(
            P("req", None), P(), P(None, "tp"), P(None, "tp"), P(None, "tp"), P("tp", None), P(),
            P(None, ("req", "tp")), P(("req", "tp"), None), P("req", "tp"), P("req", "tp"), P(), P(),
        ),
        out_specs=(P("req", "tp"), P("req", "tp"), P("req", "tp")),
        check_vma=False,
    )
```

```python
import functools
import math

import jax
import jax.numpy as jnp
from jax import lax
from jax.experimental import pallas as pl
from jax.experimental.pallas import tpu as pltpu
from jax.sharding import PartitionSpec as P

HEAD = 128
MESH = pl.DeviceIdType.MESH
NEG = -1e30
WIN = 32
CHUNK = 512
VMEM_PROJECT, VMEM_FURTHER, VMEM_TAIL = 20 << 20, 12 << 20, 20 << 20
NT = (((1,), (1,)), ((), ()))


def norm(v, g):
    center = jnp.mean(v, axis=-1, keepdims=True)
    shifted = v - center
    spread = jnp.mean(shifted * shifted, axis=-1, keepdims=True)
    return shifted * lax.rsqrt(spread + 1e-05) * g


def dot(a, b):
    return jnp.dot(a, b, preferred_element_type=jnp.float32)


def each(lo, hi, f):
    def step(i, carry):
        f(i)
        return carry

    lax.fori_loop(lo, hi, step, 0)


def line(n, me):
    side = math.isqrt(n // 2)
    y, x, c = me // (2 * side), lax.rem(me // 2, side), lax.rem(me, 2)
    far = lambda o: min(o[0], side - o[0]) + min(o[1], side - o[1])
    steps = [(i, j, k) for i in range(side) for j in range(side) for k in range(2)]
    steps = sorted(steps[1:], key=lambda o: (-far(o), -o[2]))
    ys = [lax.rem(y + i, side) for i in range(side)]
    xs = [lax.rem(x + i, side) for i in range(side)]
    cs = [c, 1 - c]
    return [(i, (ys[a] * side + xs[b]) * 2 + cs[k]) for i, (a, b, k) in enumerate(steps)]


def ring(t, z):
    steps = sorted(range(1, t), key=lambda d: -min(d, t - d))
    return [(d, lax.rem(z + d, t)) for d in steps]


def project(
    n, t, tok_h, gain_h, lens_h, order_h, wq, wk, wv, keys, values, up,
    q_all, nk, nv, tab, kb, vb, un,
    tok, gain, lens, order, wb, qs, wsem, ss, rs, us, ur,
):
    me, z = lax.axis_index("req"), lax.axis_index("tp")
    part = wq.shape[0] // 4
    small = [
        pltpu.make_async_copy(a, b, wsem.at[8 + i])
        for i, (a, b) in enumerate([(tok_h, tok), (gain_h, gain), (lens_h, lens), (order_h, order)])
    ]
    loads = [
        pltpu.make_async_copy(
            wq.at[pl.ds(i * part, part)], wb.at[0, pl.ds(i * part, part)], wsem.at[i]
        )
        for i in range(4)
    ]
    loads += [
        pltpu.make_async_copy(wk, wb.at[1], wsem.at[4]),
        pltpu.make_async_copy(wv, wb.at[2], wsem.at[5]),
        pltpu.make_async_copy(keys, kb, wsem.at[6]),
        pltpu.make_async_copy(values, vb, wsem.at[7]),
    ]
    for load in small + loads[:4]:
        load.start()
    barrier = pltpu.get_barrier_semaphore()

    others = line(n, me)
    for _, peer in others:
        pl.semaphore_signal(barrier, inc=1, device_id=(peer, z), device_id_type=MESH)
    for d in (1, t - 1):
        pl.semaphore_signal(
            barrier, inc=1, device_id=(me, lax.rem(z + d, t)), device_id_type=MESH
        )
    small[0].wait()
    small[1].wait()
    normed = norm(tok[...].astype(jnp.float32), gain[...]).astype(jnp.bfloat16)
    q = jnp.zeros((tok.shape[0], wq.shape[1]), jnp.float32)
    for i in range(4):
        loads[i].wait()
        q += dot(normed[:, i * part : (i + 1) * part], wb[0, i * part : (i + 1) * part])
    for load in loads[4:]:
        load.start()
    q = (q * HEAD**-0.5).astype(jnp.bfloat16)
    qs[...] = q
    q_all[me] = q
    pl.semaphore_wait(barrier, n + 1)
    for i, peer in others:
        pltpu.make_async_remote_copy(
            qs, q_all.at[me], ss.at[i], rs.at[me], device_id=(peer, z), device_id_type=MESH
        ).start()
    half = up.shape[0] // 2
    sides = side_copies(
        [up.at[pl.ds(i * half, half)] for i in range(2)], [un.at[i] for i in range(2)],
        us, ur, me, z, t,
    )
    for copy in sides:
        copy.start()
    loads[4].wait()
    nk[...] = dot(normed, wb[1]).astype(jnp.bfloat16)
    loads[5].wait()
    nv[...] = dot(normed, wb[2]).astype(jnp.bfloat16)
    small[2].wait()
    small[3].wait()
    m = lens.shape[1]
    sub = lax.broadcasted_iota(jnp.int32, (m, m), 0).astype(jnp.float32)
    lane = lax.broadcasted_iota(jnp.int32, (m, m), 1).astype(jnp.float32)
    len_l = lens[...].astype(jnp.float32)
    ord_s = jnp.sum(
        jnp.where(sub == lane, order[...].astype(jnp.float32), 0.0), axis=1, keepdims=True
    )
    hot = ord_s == lane
    rank = jnp.sum(jnp.where(hot, sub, 0.0), axis=0, keepdims=True)
    len_s = jnp.sum(jnp.where(hot, len_l, 0.0), axis=1, keepdims=True)
    end = jnp.sum(jnp.where(sub <= rank, len_s, 0.0), axis=0, keepdims=True)
    tab[0:1] = rank
    tab[1:2] = end - len_l
    tab[2:3] = end
    tab[3:8] = jnp.zeros((5, m), jnp.float32)


    def finish(d):
        src = lax.rem(me + d, n)
        copy = pltpu.make_async_remote_copy(
            qs, q_all.at[src], ss.at[d - 1], rs.at[src], device_id=(src, z), device_id_type=MESH
        )
        copy.wait_recv()
        copy.wait_send()

    each(1, n, finish)
    loads[6].wait()
    loads[7].wait()
    for copy in sides:
        copy.wait()


def side_copies(src, dst, ss, rs, me, z, t):
    return [
        pltpu.make_async_remote_copy(
            src[i], dst[i], ss.at[i], rs.at[i],
            device_id=(me, lax.rem(z + d, t)), device_id_type=MESH,
        )
        for i, d in enumerate((1, t - 1))
    ]


def window(slot, base, q_all, tab, kb, vb, sc, acc):
    rows, width = kb.shape
    heads = width // HEAD
    rank, first, end = tab[0:1], tab[1:2], tab[2:3]
    m = rank.shape[1]
    every_q = q_all[...].astype(jnp.float32).reshape(m, width).astype(jnp.bfloat16)
    tall = WIN * heads
    block = (
        lax.broadcasted_iota(jnp.int32, (tall, width), 0) // WIN
        == lax.broadcasted_iota(jnp.int32, (tall, width), 1) // HEAD
    )
    spot = lax.broadcasted_iota(jnp.int32, (WIN, HEAD), 1)
    pick = rank == slot + lax.broadcasted_iota(jnp.int32, (WIN, m), 0).astype(jnp.float32)
    pick = jnp.where(pick, 1.0, 0.0)
    q = dot(pick.astype(jnp.bfloat16), every_q)
    first_w = jnp.sum(pick * first, axis=1, keepdims=True) - base
    end_w = jnp.sum(pick * end, axis=1, keepdims=True) - base
    first_t = jnp.concatenate([first_w] * heads, axis=0)
    end_t = jnp.concatenate([end_w] * heads, axis=0)
    q_block = jnp.where(block, jnp.concatenate([q] * heads, axis=0), 0.0).astype(jnp.bfloat16)
    top = jnp.full((tall, HEAD), NEG, jnp.float32)
    for i in range(rows // CHUNK):
        span = slice(i * CHUNK, (i + 1) * CHUNK)
        s = lax.dot_general(q_block, kb[span], NT, preferred_element_type=jnp.float32)
        at = lax.broadcasted_iota(jnp.int32, s.shape, 1).astype(jnp.float32) + float(i * CHUNK)
        s = jnp.where(jnp.logical_and(at >= first_t, at < end_t), s, NEG)
        sc[:, span] = s
        for j in range(CHUNK // HEAD):
            top = jnp.maximum(top, s[:, j * HEAD : (j + 1) * HEAD])
    peak = jnp.max(top, axis=1, keepdims=True)
    held = jnp.zeros((tall, HEAD), jnp.float32)
    for i in range(rows // CHUNK):
        span = slice(i * CHUNK, (i + 1) * CHUNK)
        s = sc[:, span]
        e = jnp.where(s > 0.1 * NEG, jnp.exp(s - peak), 0.0)
        for j in range(CHUNK // HEAD):
            held += e[:, j * HEAD : (j + 1) * HEAD]
        o = dot(e.astype(jnp.bfloat16), vb[span])
        if i == 0:
            acc[...] = o
        else:
            acc[...] += o
    mass = jnp.sum(held, axis=1, keepdims=True)
    cut = lambda a, h: a[h * WIN : (h + 1) * WIN]
    stat = jnp.zeros((WIN, HEAD), jnp.float32)
    for h in range(heads):
        stat = jnp.where(spot == h, cut(peak, h), stat)
        stat = jnp.where(spot == heads + h, cut(mass, h), stat)
    found = jnp.concatenate(
        [acc[h * WIN : (h + 1) * WIN, h * HEAD : (h + 1) * HEAD] for h in range(heads)] + [stat],
        axis=1,
    )
    put = upright(rank) == slot + lax.broadcasted_iota(jnp.int32, (m, WIN), 1).astype(jnp.float32)
    put = jnp.where(put, 1.0, 0.0).astype(jnp.bfloat16)
    one = found.astype(jnp.bfloat16)
    rest = found - one.astype(jnp.float32)
    two = rest.astype(jnp.bfloat16)
    three = (rest - two.astype(jnp.float32)).astype(jnp.bfloat16)
    return (dot(put, one) + dot(put, two)) + dot(put, three)


def upright(row):
    m = row.shape[1]
    diag = lax.broadcasted_iota(jnp.int32, (m, m), 0) == lax.broadcasted_iota(jnp.int32, (m, m), 1)
    return jnp.sum(jnp.where(diag, row, 0.0), axis=1, keepdims=True)


def present(tab, base, rows):
    return jnp.logical_and(tab[1:2] < base + rows, tab[2:3] > base)


def further(q_all, tab, nk_in, nv_in, kb, vb, more, nk, nv, sc, acc):
    nk[...] = nk_in[...]
    nv[...] = nv_in[...]
    rows = kb.shape[0]
    base = (lax.axis_index("req") * rows).astype(jnp.float32)
    rank, here = tab[0:1], present(tab, base, rows)
    low = jnp.min(jnp.where(here, rank, 1e9)).astype(jnp.int32)
    high = jnp.max(jnp.where(here, rank, -1.0)).astype(jnp.int32)
    more[...] = jnp.zeros_like(more)

    def add(w):
        slot = (low + w * WIN).astype(jnp.float32)
        more[...] += window(slot, base, q_all, tab, kb, vb, sc, acc)

    each(1, (high - low) // WIN + 1, add)


def tail(
    n, t, more, q_all, tab, kb, vb, nk, nv, un, tok_h, gain_h, wo_h, up, down, hid,
    sc, acc, part, tok, gain, wo, got, upb, dnb, zs, zr, tp, ns, nr, ts, rr, fs, fr,
    lsem, a_s, a_r, v_s, v_r, u_s, u_r, d_s, d_r, e_s, e_r, z_s, z_r, n_s, n_r, r_s, r_r, f_s, f_r,
):
    me, z = lax.axis_index("req"), lax.axis_index("tp")
    f32, b16 = jnp.float32, jnp.bfloat16
    width = q_all.shape[2]
    heads = width // HEAD
    own, wide = tok.shape
    few = own // t
    half = up.shape[0] // 2
    loads = [
        pltpu.make_async_copy(up, upb.at[0], lsem.at[0]),
        pltpu.make_async_copy(down, dnb.at[0], lsem.at[1]),
        pltpu.make_async_copy(un.at[0], upb.at[1, pl.ds(0, half)], lsem.at[2]),
        pltpu.make_async_copy(un.at[1], upb.at[2, pl.ds(half, half)], lsem.at[3]),
        pltpu.make_async_copy(tok_h, tok, lsem.at[4]),
        pltpu.make_async_copy(gain_h, gain, lsem.at[5]),
        pltpu.make_async_copy(wo_h, wo, lsem.at[6]),
    ]
    for load in loads:
        load.start()
    barrier = pltpu.get_barrier_semaphore()

    others, others_z = line(n, me), ring(t, z)
    for _, peer in others:
        pl.semaphore_signal(barrier, inc=1, device_id=(peer, z), device_id_type=MESH)
    for _, peer in others_z:
        pl.semaphore_signal(barrier, inc=1, device_id=(me, peer), device_id_type=MESH)
    base = (me * kb.shape[0]).astype(f32)
    here = present(tab, base, kb.shape[0])
    low = jnp.min(jnp.where(here, tab[0:1], 1e9), axis=1, keepdims=True)
    found = window(low, base, q_all, tab, kb, vb, sc, acc) + more[...]
    stat = found[:, width:]
    lanes = lax.broadcasted_iota(jnp.int32, stat.shape, 1)
    here_s = upright(jnp.where(here, 1.0, 0.0)) > 0.5
    stat = jnp.where(jnp.logical_and(lanes < heads, jnp.logical_not(here_s)), NEG, stat)
    one = stat.astype(b16).astype(f32)
    two = (stat - one).astype(b16).astype(f32)
    three = (stat - one) - two
    kinds = 2 * heads
    stat = jnp.where(
        lanes < kinds,
        one,
        jnp.where(
            lanes < 2 * kinds, pltpu.roll(two, kinds, axis=1), pltpu.roll(three, 2 * kinds, axis=1)
        ),
    )
    part[:, :, :width] = found[:, :width].reshape(n, own, width).astype(b16)
    part[:, :, width:] = stat.reshape(n, own, HEAD).astype(b16)
    pl.semaphore_wait(barrier, n - 1 + t - 1)

    def line_copies(src, dst, ss, rs):
        def one(d, s, peer):
            return pltpu.make_async_remote_copy(
                src(peer), dst.at[s], ss.at[d], rs.at[s], device_id=(peer, z), device_id_type=MESH
            )

        def start():
            for i, peer in others:
                one(i, me, peer).start()

        def finish():
            def wait(d):
                other = lax.rem(me + d, n)
                copy = one(d - 1, other, other)
                copy.wait_recv()
                copy.wait_send()

            each(1, n, wait)

        return start, finish

    def z_copies(src, dst, ss, rs):
        def one(d, s, peer):
            return pltpu.make_async_remote_copy(
                src(peer), dst.at[s], ss.at[d], rs.at[s], device_id=(me, peer), device_id_type=MESH
            )

        def start():
            for d, peer in others_z:
                one(d, z, peer).start()

        def finish():
            for d, peer in others_z:
                copy = one(d, peer, peer)
                copy.wait_recv()
                copy.wait_send()

        return start, finish

    send, take = line_copies(lambda peer: part.at[peer], got, a_s, a_r)
    send()
    halves = [pl.ds(i * half, half) for i in range(2)]
    up_side = side_copies(
        [up.at[halves[1]], up.at[halves[0]]],
        [upb.at[1, halves[1]], upb.at[2, halves[0]]], v_s, v_r, me, z, t,
    )
    down_side = side_copies([down, down], [dnb.at[1], dnb.at[2]], d_s, d_r, me, z, t)
    up_relay = side_copies(
        [un.at[0], un.at[1]], [upb.at[t - 1, h] for h in halves], u_s, u_r, me, z, t
    )
    down_relay = side_copies(
        [dnb.at[1, halves[0]], dnb.at[2, halves[1]]], [dnb.at[t - 1, h] for h in halves],
        e_s, e_r, me, z, t,
    )
    for copy in down_side + up_side:
        copy.start()

    def pieces(a):
        return [
            jnp.concatenate(
                [a[k * few : (k + 1) * few, b * width : (b + 1) * width] for b in range(t)], axis=0
            )
            for k in range(t)
        ]

    q = q_all[me].astype(f32)
    kn = nk[...].astype(f32)
    vn = nv[...].astype(f32)
    spot = lax.broadcasted_iota(jnp.int32, (own, HEAD), 1)
    mine = jnp.zeros((own, HEAD), f32)
    for h in range(heads):
        cols = slice(h * HEAD, (h + 1) * HEAD)
        mine = jnp.where(spot == h, jnp.sum(q[:, cols] * kn[:, cols], axis=1, keepdims=True), mine)
    loads[4].wait()
    loads[5].wait()
    for k, piece in enumerate(pieces(tok[...].astype(f32))):
        tp[k] = piece
    gains = jnp.concatenate(
        [
            jnp.broadcast_to(gain[:, b * width : (b + 1) * width], (few, width)) for b in range(t)
        ],
        axis=0,
    )
    got[me] = part[me]
    take()
    coded = got[:, :, width:].astype(f32)
    stat = (coded + pltpu.roll(coded, HEAD - kinds, axis=2)) + pltpu.roll(
        coded, HEAD - 2 * kinds, axis=2
    )
    top = jnp.maximum(jnp.max(stat, axis=0), mine)
    scale = jnp.exp(stat - top[None])
    mass = pltpu.roll(stat, HEAD - heads, axis=2)
    self_w = jnp.exp(mine - top)
    total = self_w + jnp.sum(scale * mass, axis=0)
    attended = []
    for h in range(heads):
        cols = slice(h * HEAD, (h + 1) * HEAD)
        older = jnp.sum(got[:, :, cols].astype(f32) * scale[:, :, h : h + 1], axis=0)
        attended.append((self_w[:, h : h + 1] * vn[:, cols] + older) / total[:, h : h + 1])
    attended = jnp.concatenate(attended, axis=1).astype(b16)
    loads[6].wait()
    for k, piece in enumerate(pieces(dot(attended, wo[...]))):
        zs[k] = piece
    send, take = z_copies(lambda peer: zs.at[peer], zr, z_s, z_r)
    send()
    mid = zs[z]
    take()
    for i in range(1, t):
        mid += zr[lax.rem(z + i, t)]
    mid += tp[z]
    for copy in up_relay:
        copy.start()
    for copy in down_side:
        copy.wait()
    for copy in down_relay:
        copy.start()

    def mean(a):
        r = jnp.broadcast_to(jnp.sum(a, axis=1, keepdims=True), (own, HEAD))
        whole = r
        for b in range(1, t):
            whole += pltpu.roll(r, b * few, axis=0)
        return whole[:, :1] / wide

    shifted = mid - mean(mid)
    normed = (shifted * lax.rsqrt(mean(shifted * shifted) + 1e-05) * gains).astype(b16)
    ns[...] = normed
    nr[me] = normed
    send, take = line_copies(lambda peer: ns, nr, n_s, n_r)
    send()
    for i in (0, 2, 3):
        loads[i].wait()
    for copy in up_side + up_relay:
        copy.wait()
    take()
    rows, units = n * own, t * up.shape[0]
    row_block = lax.rem(lax.broadcasted_iota(jnp.int32, (rows, width), 0), own) // few
    x = nr[...].astype(f32).reshape(rows, width).astype(b16)
    pre = jnp.zeros((rows, units), f32)
    for b in range(t):
        y = lax.dot_general(
            x, upb[:, :, b * width : (b + 1) * width].reshape(units, width), NT,
            preferred_element_type=f32,
        )
        pre = jnp.where(row_block[:, :units] == b, y, pre)
    pre = pre.reshape(n, own, units)
    whole = pre
    for b in range(1, t):
        whole += pltpu.roll(pre, b * few, axis=1)
    act = (0.5 * whole * (1.0 + lax.erf(whole * 0.5**0.5))).reshape(rows, units).astype(b16)
    loads[1].wait()
    for copy in down_relay:
        copy.wait()
    term = jnp.zeros((rows, width), f32)
    for b in range(t):
        y = dot(act, dnb[:, :, b * width : (b + 1) * width].reshape(units, width))
        term = jnp.where(row_block == b, y, term)
    term = term.reshape(n, own, width).astype(b16)
    ts[...] = term
    send, take = line_copies(lambda peer: ts.at[peer], rr, r_s, r_r)
    send()
    rr[me] = ts[me]
    take()
    out = (mid + jnp.sum(rr[...].astype(f32), axis=0)).astype(b16)
    fs[...] = out
    fr[z] = out
    send, take = z_copies(lambda peer: fs, fr, f_s, f_r)
    send()
    take()
    every = [fr[k].astype(f32) for k in range(t)]
    final = jnp.zeros((own, width), f32)
    for b in range(t):
        rows_b = jnp.concatenate([a[b * few : (b + 1) * few] for a in every], axis=0)
        final = jnp.where(z == b, rows_b, final)
    hid[...] = final.astype(b16)


def body(
    n, t, tokens, first_gain, query_weight, key_weight, value_weight, out_weight, second_gain,
    up_weight, down_weight, cache_keys, cache_values, lengths, stream_order,
):
    f32, b16 = jnp.float32, jnp.bfloat16
    own, wide = tokens.shape
    width = query_weight.shape[1]
    requests = own * n
    units = up_weight.shape[1]
    rows = cache_keys.shape[0]
    steps = rows // CHUNK
    vmem = pl.BlockSpec(memory_space=pltpu.VMEM)
    hbm = pl.BlockSpec(memory_space=pltpu.HBM)
    dma = pltpu.SemaphoreType.DMA
    shape = jax.ShapeDtypeStruct
    up_rows = up_weight.T
    held = lambda a: pltpu.with_memory_space_constraint(a, pltpu.HBM)
    heads = width // HEAD
    q_all, nk, nv, tab, kb, vb, un = pl.pallas_call(
        functools.partial(project, n, t),
        out_shape=(
            shape((n, own, width), b16),
            shape((own, width), b16),
            shape((own, width), b16),
            shape((8, requests), f32),
            shape((rows, width), b16),
            shape((rows, width), b16),
            shape((2, units // 2, wide), b16),
        ),
        in_specs=[hbm] * 10,
        out_specs=(vmem,) * 7,
        scratch_shapes=[
            pltpu.VMEM((own, wide), b16),
            pltpu.VMEM((1, wide), f32),
            pltpu.VMEM((1, requests), jnp.int32),
            pltpu.VMEM((1, requests), jnp.int32),
            pltpu.VMEM((3, wide, width), b16),
            pltpu.VMEM((own, width), b16),
            dma((12,)),
            dma((n,)), dma((n,)),
            dma((2,)), dma((2,)),
        ],
        compiler_params=pltpu.CompilerParams(
            collective_id=0, has_side_effects=True, vmem_limit_bytes=VMEM_PROJECT
        ),
        name="project",
    )(
        *map(
            held,
            (
                tokens, first_gain.reshape(1, wide), lengths.reshape(1, requests),
                stream_order.reshape(1, requests), query_weight, key_weight, value_weight,
                cache_keys, cache_values, up_rows,
            ),
        )
    )
    more, new_keys, new_values = pl.pallas_call(
        further,
        out_shape=(
            shape((requests, width + HEAD), f32),
            shape((own, width), b16),
            shape((own, width), b16),
        ),
        in_specs=[vmem] * 6,
        out_specs=(vmem,) * 3,
        scratch_shapes=[
            pltpu.VMEM((WIN * heads, rows), f32),
            pltpu.VMEM((WIN * heads, width), f32),
        ],
        compiler_params=pltpu.CompilerParams(vmem_limit_bytes=VMEM_FURTHER),
        name="further",
    )(q_all, tab, nk, nv, kb, vb)
    hidden = pl.pallas_call(
        functools.partial(tail, n, t),
        out_shape=shape((own, width), b16),
        in_specs=[vmem] * 8 + [hbm] * 5,
        out_specs=vmem,
        scratch_shapes=[
            pltpu.VMEM((WIN * heads, rows), f32),
            pltpu.VMEM((WIN * heads, width), f32),
            pltpu.VMEM((n, own, width + HEAD), b16),
            pltpu.VMEM((own, wide), b16),
            pltpu.VMEM((1, wide), f32),
            pltpu.VMEM((width, wide), b16),
            pltpu.VMEM((n, own, width + HEAD), b16),
            pltpu.VMEM((t, units, wide), b16),
            pltpu.VMEM((t, units, wide), b16),
            pltpu.VMEM((t, own, width), f32),
            pltpu.VMEM((t, own, width), f32),
            pltpu.VMEM((t, own, width), f32),
            pltpu.VMEM((own, width), b16),
            pltpu.VMEM((n, own, width), b16),
            pltpu.VMEM((n, own, width), b16),
            pltpu.VMEM((n, own, width), b16),
            pltpu.VMEM((own, width), b16),
            pltpu.VMEM((t, own, width), b16),
            dma((7,)),
            dma((n,)), dma((n,)),
            dma((2,)), dma((2,)),
            dma((2,)), dma((2,)),
            dma((2,)), dma((2,)),
            dma((2,)), dma((2,)),
            dma((t,)), dma((t,)),
            dma((n,)), dma((n,)),
            dma((n,)), dma((n,)),
            dma((t,)), dma((t,)),
        ],
        compiler_params=pltpu.CompilerParams(
            collective_id=1, has_side_effects=True, vmem_limit_bytes=VMEM_TAIL
        ),
        name="tail",
    )(
        more, q_all, tab, kb, vb, nk, nv, un,
        *map(held, (tokens, second_gain.reshape(1, wide), out_weight, up_rows, down_weight)),
    )
    return hidden, new_keys, new_values


def solution(mesh):
    n, t = mesh.shape["req"], mesh.shape["tp"]
    return jax.shard_map(
        functools.partial(body, n, t),
        mesh=mesh,
        in_specs=(
            P("req", None), P(), P(None, "tp"), P(None, "tp"), P(None, "tp"), P("tp", None), P(),
            P(None, ("req", "tp")), P(("req", "tp"), None), P("req", "tp"), P("req", "tp"), P(), P(),
        ),
        out_specs=(P("req", "tp"), P("req", "tp"), P("req", "tp")),
        check_vma=False,
    )
```

```python
import functools
import math

import jax
import jax.numpy as jnp
from jax import lax
from jax.experimental import pallas as pl
from jax.experimental.pallas import tpu as pltpu
from jax.sharding import PartitionSpec as P

HEAD = 128
MESH = pl.DeviceIdType.MESH
NEG = -1e30
WIN = 32
CHUNK = 512
VMEM_PROJECT, VMEM_FURTHER, VMEM_TAIL = 20 << 20, 12 << 20, 20 << 20
NT = (((1,), (1,)), ((), ()))


def norm(v, g):
    center = jnp.mean(v, axis=-1, keepdims=True)
    shifted = v - center
    spread = jnp.mean(shifted * shifted, axis=-1, keepdims=True)
    return shifted * lax.rsqrt(spread + 1e-05) * g


def dot(a, b):
    return jnp.dot(a, b, preferred_element_type=jnp.float32)


def each(lo, hi, f):
    def step(i, carry):
        f(i)
        return carry

    lax.fori_loop(lo, hi, step, 0)


def line(n, me):
    side = math.isqrt(n // 2)
    y, x, c = me // (2 * side), lax.rem(me // 2, side), lax.rem(me, 2)
    far = lambda o: min(o[0], side - o[0]) + min(o[1], side - o[1])
    steps = [(i, j, k) for i in range(side) for j in range(side) for k in range(2)]
    steps = sorted(steps[1:], key=lambda o: (-far(o), -o[2]))
    ys = [lax.rem(y + i, side) for i in range(side)]
    xs = [lax.rem(x + i, side) for i in range(side)]
    cs = [c, 1 - c]
    return [(i, (ys[a] * side + xs[b]) * 2 + cs[k]) for i, (a, b, k) in enumerate(steps)]


def ring(t, z):
    steps = sorted(range(1, t), key=lambda d: -min(d, t - d))
    return [(d, lax.rem(z + d, t)) for d in steps]


def project(
    n, t, tok_h, gain_h, lens_h, order_h, wq, wk, wv, keys, values, up,
    q_all, nk, nv, tab, kb, vb, un,
    tok, gain, lens, order, wb, qs, wsem, ss, rs, us, ur,
):
    me, z = lax.axis_index("req"), lax.axis_index("tp")
    part = wq.shape[0] // 4
    small = [
        pltpu.make_async_copy(a, b, wsem.at[8 + i])
        for i, (a, b) in enumerate([(tok_h, tok), (gain_h, gain), (lens_h, lens), (order_h, order)])
    ]
    loads = [
        pltpu.make_async_copy(
            wq.at[pl.ds(i * part, part)], wb.at[0, pl.ds(i * part, part)], wsem.at[i]
        )
        for i in range(4)
    ]
    loads += [
        pltpu.make_async_copy(wk, wb.at[1], wsem.at[4]),
        pltpu.make_async_copy(wv, wb.at[2], wsem.at[5]),
        pltpu.make_async_copy(keys, kb, wsem.at[6]),
        pltpu.make_async_copy(values, vb, wsem.at[7]),
    ]
    for load in small + loads[:4]:
        load.start()
    barrier = pltpu.get_barrier_semaphore()

    others = line(n, me)
    for _, peer in others:
        pl.semaphore_signal(barrier, inc=1, device_id=(peer, z), device_id_type=MESH)
    for d in (1, t - 1):
        pl.semaphore_signal(
            barrier, inc=1, device_id=(me, lax.rem(z + d, t)), device_id_type=MESH
        )
    small[0].wait()
    small[1].wait()
    normed = norm(tok[...].astype(jnp.float32), gain[...]).astype(jnp.bfloat16)
    q = jnp.zeros((tok.shape[0], wq.shape[1]), jnp.float32)
    for i in range(4):
        loads[i].wait()
        q += dot(normed[:, i * part : (i + 1) * part], wb[0, i * part : (i + 1) * part])
    for load in loads[4:]:
        load.start()
    q = (q * HEAD**-0.5).astype(jnp.bfloat16)
    qs[...] = q
    q_all[me] = q
    pl.semaphore_wait(barrier, n + 1)
    for i, peer in others:
        pltpu.make_async_remote_copy(
            qs, q_all.at[me], ss.at[0], rs.at[0], device_id=(peer, z), device_id_type=MESH
        ).start()
    half = up.shape[0] // 2
    sides = side_copies(
        [up.at[pl.ds(i * half, half)] for i in range(2)], [un.at[i] for i in range(2)],
        us, ur, me, z, t,
    )
    for copy in sides:
        copy.start()
    loads[4].wait()
    nk[...] = dot(normed, wb[1]).astype(jnp.bfloat16)
    loads[5].wait()
    nv[...] = dot(normed, wb[2]).astype(jnp.bfloat16)
    small[2].wait()
    small[3].wait()
    m = lens.shape[1]
    sub = lax.broadcasted_iota(jnp.int32, (m, m), 0).astype(jnp.float32)
    lane = lax.broadcasted_iota(jnp.int32, (m, m), 1).astype(jnp.float32)
    len_l = lens[...].astype(jnp.float32)
    ord_s = jnp.sum(
        jnp.where(sub == lane, order[...].astype(jnp.float32), 0.0), axis=1, keepdims=True
    )
    hot = ord_s == lane
    rank = jnp.sum(jnp.where(hot, sub, 0.0), axis=0, keepdims=True)
    len_s = jnp.sum(jnp.where(hot, len_l, 0.0), axis=1, keepdims=True)
    end = jnp.sum(jnp.where(sub <= rank, len_s, 0.0), axis=0, keepdims=True)
    tab[0:1] = rank
    tab[1:2] = end - len_l
    tab[2:3] = end
    tab[3:8] = jnp.zeros((5, m), jnp.float32)

    queries = together(q_all, n - 1, ss, rs, (others[0][1], z))
    queries.wait_recv()
    queries.wait_send()
    loads[6].wait()
    loads[7].wait()
    for copy in sides:
        copy.wait()


def together(dst, count, ss, rs, device):
    slots = dst.at[pl.ds(0, count)]
    return pltpu.make_async_remote_copy(
        slots, slots, ss.at[0], rs.at[0], device_id=device, device_id_type=MESH
    )


def side_copies(src, dst, ss, rs, me, z, t):
    return [
        pltpu.make_async_remote_copy(
            src[i], dst[i], ss.at[i], rs.at[i],
            device_id=(me, lax.rem(z + d, t)), device_id_type=MESH,
        )
        for i, d in enumerate((1, t - 1))
    ]


def window(slot, base, q_all, tab, kb, vb, sc, acc):
    rows, width = kb.shape
    heads = width // HEAD
    rank, first, end = tab[0:1], tab[1:2], tab[2:3]
    m = rank.shape[1]
    every_q = q_all[...].astype(jnp.float32).reshape(m, width).astype(jnp.bfloat16)
    tall = WIN * heads
    block = (
        lax.broadcasted_iota(jnp.int32, (tall, width), 0) // WIN
        == lax.broadcasted_iota(jnp.int32, (tall, width), 1) // HEAD
    )
    spot = lax.broadcasted_iota(jnp.int32, (WIN, HEAD), 1)
    pick = rank == slot + lax.broadcasted_iota(jnp.int32, (WIN, m), 0).astype(jnp.float32)
    pick = jnp.where(pick, 1.0, 0.0)
    q = dot(pick.astype(jnp.bfloat16), every_q)
    first_w = jnp.sum(pick * first, axis=1, keepdims=True) - base
    end_w = jnp.sum(pick * end, axis=1, keepdims=True) - base
    first_t = jnp.concatenate([first_w] * heads, axis=0)
    end_t = jnp.concatenate([end_w] * heads, axis=0)
    q_block = jnp.where(block, jnp.concatenate([q] * heads, axis=0), 0.0).astype(jnp.bfloat16)
    top = jnp.full((tall, HEAD), NEG, jnp.float32)
    for i in range(rows // CHUNK):
        span = slice(i * CHUNK, (i + 1) * CHUNK)
        s = lax.dot_general(q_block, kb[span], NT, preferred_element_type=jnp.float32)
        at = lax.broadcasted_iota(jnp.int32, s.shape, 1).astype(jnp.float32) + float(i * CHUNK)
        s = jnp.where(jnp.logical_and(at >= first_t, at < end_t), s, NEG)
        sc[:, span] = s
        for j in range(CHUNK // HEAD):
            top = jnp.maximum(top, s[:, j * HEAD : (j + 1) * HEAD])
    peak = jnp.max(top, axis=1, keepdims=True)
    held = jnp.zeros((tall, HEAD), jnp.float32)
    for i in range(rows // CHUNK):
        span = slice(i * CHUNK, (i + 1) * CHUNK)
        s = sc[:, span]
        e = jnp.where(s > 0.1 * NEG, jnp.exp(s - peak), 0.0)
        for j in range(CHUNK // HEAD):
            held += e[:, j * HEAD : (j + 1) * HEAD]
        o = dot(e.astype(jnp.bfloat16), vb[span])
        if i == 0:
            acc[...] = o
        else:
            acc[...] += o
    mass = jnp.sum(held, axis=1, keepdims=True)
    cut = lambda a, h: a[h * WIN : (h + 1) * WIN]
    stat = jnp.zeros((WIN, HEAD), jnp.float32)
    for h in range(heads):
        stat = jnp.where(spot == h, cut(peak, h), stat)
        stat = jnp.where(spot == heads + h, cut(mass, h), stat)
    found = jnp.concatenate(
        [acc[h * WIN : (h + 1) * WIN, h * HEAD : (h + 1) * HEAD] for h in range(heads)] + [stat],
        axis=1,
    )
    put = upright(rank) == slot + lax.broadcasted_iota(jnp.int32, (m, WIN), 1).astype(jnp.float32)
    put = jnp.where(put, 1.0, 0.0).astype(jnp.bfloat16)
    one = found.astype(jnp.bfloat16)
    rest = found - one.astype(jnp.float32)
    two = rest.astype(jnp.bfloat16)
    three = (rest - two.astype(jnp.float32)).astype(jnp.bfloat16)
    return (dot(put, one) + dot(put, two)) + dot(put, three)


def upright(row):
    m = row.shape[1]
    diag = lax.broadcasted_iota(jnp.int32, (m, m), 0) == lax.broadcasted_iota(jnp.int32, (m, m), 1)
    return jnp.sum(jnp.where(diag, row, 0.0), axis=1, keepdims=True)


def present(tab, base, rows):
    return jnp.logical_and(tab[1:2] < base + rows, tab[2:3] > base)


def further(q_all, tab, nk_in, nv_in, kb, vb, more, nk, nv, sc, acc):
    nk[...] = nk_in[...]
    nv[...] = nv_in[...]
    rows = kb.shape[0]
    base = (lax.axis_index("req") * rows).astype(jnp.float32)
    rank, here = tab[0:1], present(tab, base, rows)
    low = jnp.min(jnp.where(here, rank, 1e9)).astype(jnp.int32)
    high = jnp.max(jnp.where(here, rank, -1.0)).astype(jnp.int32)
    more[...] = jnp.zeros_like(more)

    def add(w):
        slot = (low + w * WIN).astype(jnp.float32)
        more[...] += window(slot, base, q_all, tab, kb, vb, sc, acc)

    each(1, (high - low) // WIN + 1, add)


def tail(
    n, t, more, q_all, tab, kb, vb, nk, nv, un, tok_h, gain_h, wo_h, up, down, hid,
    sc, acc, part, tok, gain, wo, got, upb, dnb, zs, zr, tp, ns, nr, ts, rr, fs, fr,
    lsem, a_s, a_r, v_s, v_r, u_s, u_r, d_s, d_r, e_s, e_r, z_s, z_r, n_s, n_r, r_s, r_r, f_s, f_r,
):
    me, z = lax.axis_index("req"), lax.axis_index("tp")
    f32, b16 = jnp.float32, jnp.bfloat16
    width = q_all.shape[2]
    heads = width // HEAD
    own, wide = tok.shape
    few = own // t
    half = up.shape[0] // 2
    loads = [
        pltpu.make_async_copy(up, upb.at[0], lsem.at[0]),
        pltpu.make_async_copy(down, dnb.at[0], lsem.at[1]),
        pltpu.make_async_copy(un.at[0], upb.at[1, pl.ds(0, half)], lsem.at[2]),
        pltpu.make_async_copy(un.at[1], upb.at[2, pl.ds(half, half)], lsem.at[3]),
        pltpu.make_async_copy(tok_h, tok, lsem.at[4]),
        pltpu.make_async_copy(gain_h, gain, lsem.at[5]),
        pltpu.make_async_copy(wo_h, wo, lsem.at[6]),
    ]
    for load in loads:
        load.start()
    barrier = pltpu.get_barrier_semaphore()

    others, others_z = line(n, me), ring(t, z)
    for _, peer in others:
        pl.semaphore_signal(barrier, inc=1, device_id=(peer, z), device_id_type=MESH)
    for _, peer in others_z:
        pl.semaphore_signal(barrier, inc=1, device_id=(me, peer), device_id_type=MESH)
    base = (me * kb.shape[0]).astype(f32)
    here = present(tab, base, kb.shape[0])
    low = jnp.min(jnp.where(here, tab[0:1], 1e9), axis=1, keepdims=True)
    found = window(low, base, q_all, tab, kb, vb, sc, acc) + more[...]
    stat = found[:, width:]
    lanes = lax.broadcasted_iota(jnp.int32, stat.shape, 1)
    here_s = upright(jnp.where(here, 1.0, 0.0)) > 0.5
    stat = jnp.where(jnp.logical_and(lanes < heads, jnp.logical_not(here_s)), NEG, stat)
    one = stat.astype(b16).astype(f32)
    two = (stat - one).astype(b16).astype(f32)
    three = (stat - one) - two
    kinds = 2 * heads
    stat = jnp.where(
        lanes < kinds,
        one,
        jnp.where(
            lanes < 2 * kinds, pltpu.roll(two, kinds, axis=1), pltpu.roll(three, 2 * kinds, axis=1)
        ),
    )
    part[:, :, :width] = found[:, :width].reshape(n, own, width).astype(b16)
    part[:, :, width:] = stat.reshape(n, own, HEAD).astype(b16)
    pl.semaphore_wait(barrier, n - 1 + t - 1)

    sent = []

    def line_copies(src, dst, ss, rs):
        def start():
            for _, peer in others:
                pltpu.make_async_remote_copy(
                    src(peer), dst.at[me], ss.at[0], rs.at[0],
                    device_id=(peer, z), device_id_type=MESH,
                ).start()

        whole = together(dst, n - 1, ss, rs, (others[0][1], z))
        sent.append(whole)
        return start, whole.wait_recv

    def z_copies(src, dst, ss, rs):
        def start():
            for _, peer in others_z:
                pltpu.make_async_remote_copy(
                    src(peer), dst.at[z], ss.at[0], rs.at[0],
                    device_id=(me, peer), device_id_type=MESH,
                ).start()

        whole = together(dst, t - 1, ss, rs, (me, others_z[0][1]))
        sent.append(whole)
        return start, whole.wait_recv

    send, take = line_copies(lambda peer: part.at[peer], got, a_s, a_r)
    send()
    halves = [pl.ds(i * half, half) for i in range(2)]
    up_side = side_copies(
        [up.at[halves[1]], up.at[halves[0]]],
        [upb.at[1, halves[1]], upb.at[2, halves[0]]], v_s, v_r, me, z, t,
    )
    down_side = side_copies([down, down], [dnb.at[1], dnb.at[2]], d_s, d_r, me, z, t)
    up_relay = side_copies(
        [un.at[0], un.at[1]], [upb.at[t - 1, h] for h in halves], u_s, u_r, me, z, t
    )
    down_relay = side_copies(
        [dnb.at[1, halves[0]], dnb.at[2, halves[1]]], [dnb.at[t - 1, h] for h in halves],
        e_s, e_r, me, z, t,
    )
    for copy in down_side + up_side:
        copy.start()

    def pieces(a):
        return [
            jnp.concatenate(
                [a[k * few : (k + 1) * few, b * width : (b + 1) * width] for b in range(t)], axis=0
            )
            for k in range(t)
        ]

    q = q_all[me].astype(f32)
    kn = nk[...].astype(f32)
    vn = nv[...].astype(f32)
    spot = lax.broadcasted_iota(jnp.int32, (own, HEAD), 1)
    mine = jnp.zeros((own, HEAD), f32)
    for h in range(heads):
        cols = slice(h * HEAD, (h + 1) * HEAD)
        mine = jnp.where(spot == h, jnp.sum(q[:, cols] * kn[:, cols], axis=1, keepdims=True), mine)
    loads[4].wait()
    loads[5].wait()
    for k, piece in enumerate(pieces(tok[...].astype(f32))):
        tp[k] = piece
    gains = jnp.concatenate(
        [
            jnp.broadcast_to(gain[:, b * width : (b + 1) * width], (few, width)) for b in range(t)
        ],
        axis=0,
    )
    got[me] = part[me]
    take()
    coded = got[:, :, width:].astype(f32)
    stat = (coded + pltpu.roll(coded, HEAD - kinds, axis=2)) + pltpu.roll(
        coded, HEAD - 2 * kinds, axis=2
    )
    top = jnp.maximum(jnp.max(stat, axis=0), mine)
    scale = jnp.exp(stat - top[None])
    mass = pltpu.roll(stat, HEAD - heads, axis=2)
    self_w = jnp.exp(mine - top)
    total = self_w + jnp.sum(scale * mass, axis=0)
    attended = []
    for h in range(heads):
        cols = slice(h * HEAD, (h + 1) * HEAD)
        older = jnp.sum(got[:, :, cols].astype(f32) * scale[:, :, h : h + 1], axis=0)
        attended.append((self_w[:, h : h + 1] * vn[:, cols] + older) / total[:, h : h + 1])
    attended = jnp.concatenate(attended, axis=1).astype(b16)
    loads[6].wait()
    for k, piece in enumerate(pieces(dot(attended, wo[...]))):
        zs[k] = piece
    send, take = z_copies(lambda peer: zs.at[peer], zr, z_s, z_r)
    send()
    mid = zs[z]
    take()
    for i in range(1, t):
        mid += zr[lax.rem(z + i, t)]
    mid += tp[z]
    for copy in up_relay:
        copy.start()
    for copy in down_side:
        copy.wait()
    for copy in down_relay:
        copy.start()

    def mean(a):
        r = jnp.broadcast_to(jnp.sum(a, axis=1, keepdims=True), (own, HEAD))
        whole = r
        for b in range(1, t):
            whole += pltpu.roll(r, b * few, axis=0)
        return whole[:, :1] / wide

    shifted = mid - mean(mid)
    normed = (shifted * lax.rsqrt(mean(shifted * shifted) + 1e-05) * gains).astype(b16)
    ns[...] = normed
    nr[me] = normed
    send, take = line_copies(lambda peer: ns, nr, n_s, n_r)
    send()
    for i in (0, 2, 3):
        loads[i].wait()
    for copy in up_side + up_relay:
        copy.wait()
    take()
    rows, units = n * own, t * up.shape[0]
    row_block = lax.rem(lax.broadcasted_iota(jnp.int32, (rows, width), 0), own) // few
    x = nr[...].astype(f32).reshape(rows, width).astype(b16)
    pre = jnp.zeros((rows, units), f32)
    for b in range(t):
        y = lax.dot_general(
            x, upb[:, :, b * width : (b + 1) * width].reshape(units, width), NT,
            preferred_element_type=f32,
        )
        pre = jnp.where(row_block[:, :units] == b, y, pre)
    pre = pre.reshape(n, own, units)
    whole = pre
    for b in range(1, t):
        whole += pltpu.roll(pre, b * few, axis=1)
    act = (0.5 * whole * (1.0 + lax.erf(whole * 0.5**0.5))).reshape(rows, units).astype(b16)
    loads[1].wait()
    for copy in down_relay:
        copy.wait()
    term = jnp.zeros((rows, width), f32)
    for b in range(t):
        y = dot(act, dnb[:, :, b * width : (b + 1) * width].reshape(units, width))
        term = jnp.where(row_block == b, y, term)
    term = term.reshape(n, own, width).astype(b16)
    ts[...] = term
    send, take = line_copies(lambda peer: ts.at[peer], rr, r_s, r_r)
    send()
    rr[me] = ts[me]
    take()
    out = (mid + jnp.sum(rr[...].astype(f32), axis=0)).astype(b16)
    fs[...] = out
    fr[z] = out
    send, take = z_copies(lambda peer: fs, fr, f_s, f_r)
    send()
    take()
    every = [fr[k].astype(f32) for k in range(t)]
    final = jnp.zeros((own, width), f32)
    for b in range(t):
        rows_b = jnp.concatenate([a[b * few : (b + 1) * few] for a in every], axis=0)
        final = jnp.where(z == b, rows_b, final)
    hid[...] = final.astype(b16)
    for copies in sent:
        copies.wait_send()


def body(
    n, t, tokens, first_gain, query_weight, key_weight, value_weight, out_weight, second_gain,
    up_weight, down_weight, cache_keys, cache_values, lengths, stream_order,
):
    f32, b16 = jnp.float32, jnp.bfloat16
    own, wide = tokens.shape
    width = query_weight.shape[1]
    requests = own * n
    units = up_weight.shape[1]
    rows = cache_keys.shape[0]
    steps = rows // CHUNK
    vmem = pl.BlockSpec(memory_space=pltpu.VMEM)
    hbm = pl.BlockSpec(memory_space=pltpu.HBM)
    dma = pltpu.SemaphoreType.DMA
    shape = jax.ShapeDtypeStruct
    up_rows = up_weight.T
    held = lambda a: pltpu.with_memory_space_constraint(a, pltpu.HBM)
    heads = width // HEAD
    q_all, nk, nv, tab, kb, vb, un = pl.pallas_call(
        functools.partial(project, n, t),
        out_shape=(
            shape((n, own, width), b16),
            shape((own, width), b16),
            shape((own, width), b16),
            shape((8, requests), f32),
            shape((rows, width), b16),
            shape((rows, width), b16),
            shape((2, units // 2, wide), b16),
        ),
        in_specs=[hbm] * 10,
        out_specs=(vmem,) * 7,
        scratch_shapes=[
            pltpu.VMEM((own, wide), b16),
            pltpu.VMEM((1, wide), f32),
            pltpu.VMEM((1, requests), jnp.int32),
            pltpu.VMEM((1, requests), jnp.int32),
            pltpu.VMEM((3, wide, width), b16),
            pltpu.VMEM((own, width), b16),
            dma((12,)),
            dma((1,)), dma((1,)),
            dma((2,)), dma((2,)),
        ],
        compiler_params=pltpu.CompilerParams(
            collective_id=0, has_side_effects=True, vmem_limit_bytes=VMEM_PROJECT
        ),
        name="project",
    )(
        *map(
            held,
            (
                tokens, first_gain.reshape(1, wide), lengths.reshape(1, requests),
                stream_order.reshape(1, requests), query_weight, key_weight, value_weight,
                cache_keys, cache_values, up_rows,
            ),
        )
    )
    more, new_keys, new_values = pl.pallas_call(
        further,
        out_shape=(
            shape((requests, width + HEAD), f32),
            shape((own, width), b16),
            shape((own, width), b16),
        ),
        in_specs=[vmem] * 6,
        out_specs=(vmem,) * 3,
        scratch_shapes=[
            pltpu.VMEM((WIN * heads, rows), f32),
            pltpu.VMEM((WIN * heads, width), f32),
        ],
        compiler_params=pltpu.CompilerParams(vmem_limit_bytes=VMEM_FURTHER),
        name="further",
    )(q_all, tab, nk, nv, kb, vb)
    hidden = pl.pallas_call(
        functools.partial(tail, n, t),
        out_shape=shape((own, width), b16),
        in_specs=[vmem] * 8 + [hbm] * 5,
        out_specs=vmem,
        scratch_shapes=[
            pltpu.VMEM((WIN * heads, rows), f32),
            pltpu.VMEM((WIN * heads, width), f32),
            pltpu.VMEM((n, own, width + HEAD), b16),
            pltpu.VMEM((own, wide), b16),
            pltpu.VMEM((1, wide), f32),
            pltpu.VMEM((width, wide), b16),
            pltpu.VMEM((n, own, width + HEAD), b16),
            pltpu.VMEM((t, units, wide), b16),
            pltpu.VMEM((t, units, wide), b16),
            pltpu.VMEM((t, own, width), f32),
            pltpu.VMEM((t, own, width), f32),
            pltpu.VMEM((t, own, width), f32),
            pltpu.VMEM((own, width), b16),
            pltpu.VMEM((n, own, width), b16),
            pltpu.VMEM((n, own, width), b16),
            pltpu.VMEM((n, own, width), b16),
            pltpu.VMEM((own, width), b16),
            pltpu.VMEM((t, own, width), b16),
            dma((7,)),
            dma((1,)), dma((1,)),
            dma((2,)), dma((2,)),
            dma((2,)), dma((2,)),
            dma((2,)), dma((2,)),
            dma((2,)), dma((2,)),
            dma((1,)), dma((1,)),
            dma((1,)), dma((1,)),
            dma((1,)), dma((1,)),
            dma((1,)), dma((1,)),
        ],
        compiler_params=pltpu.CompilerParams(
            collective_id=1, has_side_effects=True, vmem_limit_bytes=VMEM_TAIL
        ),
        name="tail",
    )(
        more, q_all, tab, kb, vb, nk, nv, un,
        *map(held, (tokens, second_gain.reshape(1, wide), out_weight, up_rows, down_weight)),
    )
    return hidden, new_keys, new_values


def solution(mesh):
    n, t = mesh.shape["req"], mesh.shape["tp"]
    return jax.shard_map(
        functools.partial(body, n, t),
        mesh=mesh,
        in_specs=(
            P("req", None), P(), P(None, "tp"), P(None, "tp"), P(None, "tp"), P("tp", None), P(),
            P(None, ("req", "tp")), P(("req", "tp"), None), P("req", "tp"), P("req", "tp"), P(), P(),
        ),
        out_specs=(P("req", "tp"), P("req", "tp"), P("req", "tp")),
        check_vma=False,
    )
```

```python
import functools
import math

import jax
import jax.numpy as jnp
from jax import lax
from jax.experimental import pallas as pl
from jax.experimental.pallas import tpu as pltpu
from jax.sharding import PartitionSpec as P

HEAD = 128
MESH = pl.DeviceIdType.MESH
NEG = -1e30
WIN = 32
CHUNK = 512
VMEM_PROJECT, VMEM_FURTHER, VMEM_TAIL = 20 << 20, 12 << 20, 20 << 20
NT = (((1,), (1,)), ((), ()))


def norm(v, g):
    center = jnp.mean(v, axis=-1, keepdims=True)
    shifted = v - center
    spread = jnp.mean(shifted * shifted, axis=-1, keepdims=True)
    return shifted * lax.rsqrt(spread + 1e-05) * g


def dot(a, b):
    return jnp.dot(a, b, preferred_element_type=jnp.float32)


def each(lo, hi, f):
    def step(i, carry):
        f(i)
        return carry

    lax.fori_loop(lo, hi, step, 0)


def line(n, me):
    side = math.isqrt(n // 2)
    y, x, c = me // (2 * side), lax.rem(me // 2, side), lax.rem(me, 2)
    far = lambda o: min(o[0], side - o[0]) + min(o[1], side - o[1])
    steps = [(i, j, k) for i in range(side) for j in range(side) for k in range(2)]
    steps = sorted(steps[1:], key=lambda o: (-far(o), -o[2]))
    ys = [lax.rem(y + i, side) for i in range(side)]
    xs = [lax.rem(x + i, side) for i in range(side)]
    cs = [c, 1 - c]
    return [(i, (ys[a] * side + xs[b]) * 2 + cs[k]) for i, (a, b, k) in enumerate(steps)]


def ring(t, z):
    steps = sorted(range(1, t), key=lambda d: -min(d, t - d))
    return [(d, lax.rem(z + d, t)) for d in steps]


def project(
    n, t, tok_h, gain_h, lens_h, order_h, wq, wk, wv, keys, values, up,
    q_all, nk, nv, tab, kb, vb, un,
    tok, gain, lens, order, wb, qs, wsem, ss, rs, us, ur,
):
    me, z = lax.axis_index("req"), lax.axis_index("tp")
    part = wq.shape[0] // 4
    small = [
        pltpu.make_async_copy(a, b, wsem.at[8 + i])
        for i, (a, b) in enumerate([(tok_h, tok), (gain_h, gain), (lens_h, lens), (order_h, order)])
    ]
    loads = [
        pltpu.make_async_copy(
            wq.at[pl.ds(i * part, part)], wb.at[0, pl.ds(i * part, part)], wsem.at[i]
        )
        for i in range(4)
    ]
    loads += [
        pltpu.make_async_copy(wk, wb.at[1], wsem.at[4]),
        pltpu.make_async_copy(wv, wb.at[2], wsem.at[5]),
        pltpu.make_async_copy(keys, kb, wsem.at[6]),
        pltpu.make_async_copy(values, vb, wsem.at[7]),
    ]
    for load in small + loads[:4]:
        load.start()
    barrier = pltpu.get_barrier_semaphore()

    others = line(n, me)
    for _, peer in others:
        pl.semaphore_signal(barrier, inc=1, device_id=(peer, z), device_id_type=MESH)
    for d in (1, t - 1):
        pl.semaphore_signal(
            barrier, inc=1, device_id=(me, lax.rem(z + d, t)), device_id_type=MESH
        )
    small[0].wait()
    small[1].wait()
    normed = norm(tok[...].astype(jnp.float32), gain[...]).astype(jnp.bfloat16)
    q = jnp.zeros((tok.shape[0], wq.shape[1]), jnp.float32)
    for i in range(4):
        loads[i].wait()
        q += dot(normed[:, i * part : (i + 1) * part], wb[0, i * part : (i + 1) * part])
    for load in loads[4:]:
        load.start()
    q = (q * HEAD**-0.5).astype(jnp.bfloat16)
    qs[...] = q
    q_all[me] = q
    pl.semaphore_wait(barrier, n + 1)
    for i, peer in others:
        pltpu.make_async_remote_copy(
            qs, q_all.at[me], ss.at[0], rs.at[0], device_id=(peer, z), device_id_type=MESH
        ).start()
    half = up.shape[0] // 2
    sides = side_copies(
        [up.at[pl.ds(i * half, half)] for i in range(2)], [un.at[i] for i in range(2)],
        us, ur, me, z, t,
    )
    for copy in sides:
        copy.start()
    loads[4].wait()
    nk[...] = dot(normed, wb[1]).astype(jnp.bfloat16)
    loads[5].wait()
    nv[...] = dot(normed, wb[2]).astype(jnp.bfloat16)
    small[2].wait()
    small[3].wait()
    m = lens.shape[1]
    sub = lax.broadcasted_iota(jnp.int32, (m, m), 0).astype(jnp.float32)
    lane = lax.broadcasted_iota(jnp.int32, (m, m), 1).astype(jnp.float32)
    len_l = lens[...].astype(jnp.float32)
    ord_s = jnp.sum(
        jnp.where(sub == lane, order[...].astype(jnp.float32), 0.0), axis=1, keepdims=True
    )
    hot = ord_s == lane
    rank = jnp.sum(jnp.where(hot, sub, 0.0), axis=0, keepdims=True)
    len_s = jnp.sum(jnp.where(hot, len_l, 0.0), axis=1, keepdims=True)
    end = jnp.sum(jnp.where(sub <= rank, len_s, 0.0), axis=0, keepdims=True)
    tab[0:1] = rank
    tab[1:2] = end - len_l
    tab[2:3] = end
    tab[3:8] = jnp.zeros((5, m), jnp.float32)

    queries = together(q_all, n - 1, ss, rs, (others[0][1], z))
    queries.wait_recv()
    queries.wait_send()
    loads[6].wait()
    loads[7].wait()
    for copy in sides:
        copy.wait()


def together(dst, count, ss, rs, device):
    slots = dst.at[pl.ds(0, count)]
    return pltpu.make_async_remote_copy(
        slots, slots, ss.at[0], rs.at[0], device_id=device, device_id_type=MESH
    )


def side_copies(src, dst, ss, rs, me, z, t):
    return [
        pltpu.make_async_remote_copy(
            src[i], dst[i], ss.at[i], rs.at[i],
            device_id=(me, lax.rem(z + d, t)), device_id_type=MESH,
        )
        for i, d in enumerate((1, t - 1))
    ]


def window(slot, base, q_all, tab, kb, vb, sc, acc):
    rows, width = kb.shape
    heads = width // HEAD
    rank, first, end = tab[0:1], tab[1:2], tab[2:3]
    m = rank.shape[1]
    every_q = q_all[...].astype(jnp.float32).reshape(m, width).astype(jnp.bfloat16)
    tall = WIN * heads
    block = (
        lax.broadcasted_iota(jnp.int32, (tall, width), 0) // WIN
        == lax.broadcasted_iota(jnp.int32, (tall, width), 1) // HEAD
    )
    spot = lax.broadcasted_iota(jnp.int32, (WIN, HEAD), 1)
    pick = rank == slot + lax.broadcasted_iota(jnp.int32, (WIN, m), 0).astype(jnp.float32)
    pick = jnp.where(pick, 1.0, 0.0)
    q = dot(pick.astype(jnp.bfloat16), every_q)
    first_w = jnp.sum(pick * first, axis=1, keepdims=True) - base
    end_w = jnp.sum(pick * end, axis=1, keepdims=True) - base
    first_t = jnp.concatenate([first_w] * heads, axis=0)
    end_t = jnp.concatenate([end_w] * heads, axis=0)
    q_block = jnp.where(block, jnp.concatenate([q] * heads, axis=0), 0.0).astype(jnp.bfloat16)
    top = jnp.full((tall, HEAD), NEG, jnp.float32)
    at = lax.broadcasted_iota(jnp.int32, (tall, CHUNK), 1).astype(jnp.float32)
    for i in range(rows // CHUNK):
        span = slice(i * CHUNK, (i + 1) * CHUNK)
        s = lax.dot_general(q_block, kb[span], NT, preferred_element_type=jnp.float32)
        off = float(i * CHUNK)
        s = jnp.where(jnp.logical_and(at >= first_t - off, at < end_t - off), s, NEG)
        sc[:, span] = s
        for j in range(CHUNK // HEAD):
            top = jnp.maximum(top, s[:, j * HEAD : (j + 1) * HEAD])
    peak = jnp.max(top, axis=1, keepdims=True)
    held = jnp.zeros((tall, HEAD), jnp.float32)
    level = jnp.maximum(peak, 0.1 * NEG)
    for i in range(rows // CHUNK):
        span = slice(i * CHUNK, (i + 1) * CHUNK)
        s = sc[:, span]
        e = jnp.exp(s - level)
        for j in range(CHUNK // HEAD):
            held += e[:, j * HEAD : (j + 1) * HEAD]
        o = dot(e.astype(jnp.bfloat16), vb[span])
        if i == 0:
            acc[...] = o
        else:
            acc[...] += o
    mass = jnp.sum(held, axis=1, keepdims=True)
    cut = lambda a, h: a[h * WIN : (h + 1) * WIN]
    stat = jnp.zeros((WIN, HEAD), jnp.float32)
    for h in range(heads):
        stat = jnp.where(spot == h, cut(peak, h), stat)
        stat = jnp.where(spot == heads + h, cut(mass, h), stat)
    found = jnp.concatenate(
        [acc[h * WIN : (h + 1) * WIN, h * HEAD : (h + 1) * HEAD] for h in range(heads)] + [stat],
        axis=1,
    )
    put = upright(rank) == slot + lax.broadcasted_iota(jnp.int32, (m, WIN), 1).astype(jnp.float32)
    put = jnp.where(put, 1.0, 0.0).astype(jnp.bfloat16)
    one = found.astype(jnp.bfloat16)
    rest = stat - one[:, width:].astype(jnp.float32)
    two = rest.astype(jnp.bfloat16)
    three = (rest - two.astype(jnp.float32)).astype(jnp.bfloat16)
    exact = (dot(put, one[:, width:]) + dot(put, two)) + dot(put, three)
    return jnp.concatenate([dot(put, one[:, :width]), exact], axis=1)


def upright(row):
    m = row.shape[1]
    diag = lax.broadcasted_iota(jnp.int32, (m, m), 0) == lax.broadcasted_iota(jnp.int32, (m, m), 1)
    return jnp.sum(jnp.where(diag, row, 0.0), axis=1, keepdims=True)


def present(tab, base, rows):
    return jnp.logical_and(tab[1:2] < base + rows, tab[2:3] > base)


def further(q_all, tab, nk_in, nv_in, kb, vb, more, nk, nv, sc, acc):
    nk[...] = nk_in[...]
    nv[...] = nv_in[...]
    rows = kb.shape[0]
    base = (lax.axis_index("req") * rows).astype(jnp.float32)
    rank, here = tab[0:1], present(tab, base, rows)
    low = jnp.min(jnp.where(here, rank, 1e9)).astype(jnp.int32)
    high = jnp.max(jnp.where(here, rank, -1.0)).astype(jnp.int32)
    more[...] = jnp.zeros_like(more)

    def add(w):
        slot = (low + w * WIN).astype(jnp.float32)
        more[...] += window(slot, base, q_all, tab, kb, vb, sc, acc)

    each(1, (high - low) // WIN + 1, add)


def tail(
    n, t, more, q_all, tab, kb, vb, nk, nv, un, tok_h, gain_h, wo_h, up, down, hid,
    sc, acc, part, tok, gain, wo, got, upb, dnb, zs, zr, tp, ns, nr, ts, rr, fs, fr,
    lsem, a_s, a_r, v_s, v_r, u_s, u_r, d_s, d_r, e_s, e_r, z_s, z_r, n_s, n_r, r_s, r_r, f_s, f_r,
):
    me, z = lax.axis_index("req"), lax.axis_index("tp")
    f32, b16 = jnp.float32, jnp.bfloat16
    width = q_all.shape[2]
    heads = width // HEAD
    own, wide = tok.shape
    few = own // t
    half = up.shape[0] // 2
    loads = [
        pltpu.make_async_copy(up, upb.at[0], lsem.at[0]),
        pltpu.make_async_copy(down, dnb.at[0], lsem.at[1]),
        pltpu.make_async_copy(un.at[0], upb.at[1, pl.ds(0, half)], lsem.at[2]),
        pltpu.make_async_copy(un.at[1], upb.at[2, pl.ds(half, half)], lsem.at[3]),
        pltpu.make_async_copy(tok_h, tok, lsem.at[4]),
        pltpu.make_async_copy(gain_h, gain, lsem.at[5]),
        pltpu.make_async_copy(wo_h, wo, lsem.at[6]),
    ]
    for load in loads:
        load.start()
    barrier = pltpu.get_barrier_semaphore()

    others, others_z = line(n, me), ring(t, z)
    for _, peer in others:
        pl.semaphore_signal(barrier, inc=1, device_id=(peer, z), device_id_type=MESH)
    for _, peer in others_z:
        pl.semaphore_signal(barrier, inc=1, device_id=(me, peer), device_id_type=MESH)
    base = (me * kb.shape[0]).astype(f32)
    here = present(tab, base, kb.shape[0])
    low = jnp.min(jnp.where(here, tab[0:1], 1e9), axis=1, keepdims=True)
    found = window(low, base, q_all, tab, kb, vb, sc, acc) + more[...]
    stat = found[:, width:]
    lanes = lax.broadcasted_iota(jnp.int32, stat.shape, 1)
    here_s = upright(jnp.where(here, 1.0, 0.0)) > 0.5
    stat = jnp.where(jnp.logical_and(lanes < heads, jnp.logical_not(here_s)), NEG, stat)
    one = stat.astype(b16).astype(f32)
    two = (stat - one).astype(b16).astype(f32)
    three = (stat - one) - two
    kinds = 2 * heads
    stat = jnp.where(
        lanes < kinds,
        one,
        jnp.where(
            lanes < 2 * kinds, pltpu.roll(two, kinds, axis=1), pltpu.roll(three, 2 * kinds, axis=1)
        ),
    )
    part[:, :, :width] = found[:, :width].reshape(n, own, width).astype(b16)
    part[:, :, width:] = stat.reshape(n, own, HEAD).astype(b16)
    pl.semaphore_wait(barrier, n - 1 + t - 1)

    sent = []

    def line_copies(src, dst, ss, rs):
        def start():
            for _, peer in others:
                pltpu.make_async_remote_copy(
                    src(peer), dst.at[me], ss.at[0], rs.at[0],
                    device_id=(peer, z), device_id_type=MESH,
                ).start()

        whole = together(dst, n - 1, ss, rs, (others[0][1], z))
        sent.append(whole)
        return start, whole.wait_recv

    def z_copies(src, dst, ss, rs):
        def start():
            for _, peer in others_z:
                pltpu.make_async_remote_copy(
                    src(peer), dst.at[z], ss.at[0], rs.at[0],
                    device_id=(me, peer), device_id_type=MESH,
                ).start()

        whole = together(dst, t - 1, ss, rs, (me, others_z[0][1]))
        sent.append(whole)
        return start, whole.wait_recv

    send, take = line_copies(lambda peer: part.at[peer], got, a_s, a_r)
    send()
    halves = [pl.ds(i * half, half) for i in range(2)]
    up_side = side_copies(
        [up.at[halves[1]], up.at[halves[0]]],
        [upb.at[1, halves[1]], upb.at[2, halves[0]]], v_s, v_r, me, z, t,
    )
    down_side = side_copies([down, down], [dnb.at[1], dnb.at[2]], d_s, d_r, me, z, t)
    up_relay = side_copies(
        [un.at[0], un.at[1]], [upb.at[t - 1, h] for h in halves], u_s, u_r, me, z, t
    )
    down_relay = side_copies(
        [dnb.at[1, halves[0]], dnb.at[2, halves[1]]], [dnb.at[t - 1, h] for h in halves],
        e_s, e_r, me, z, t,
    )
    for copy in down_side + up_side:
        copy.start()

    def pieces(a):
        return [
            jnp.concatenate(
                [a[k * few : (k + 1) * few, b * width : (b + 1) * width] for b in range(t)], axis=0
            )
            for k in range(t)
        ]

    q = q_all[me].astype(f32)
    kn = nk[...].astype(f32)
    vn = nv[...].astype(f32)
    spot = lax.broadcasted_iota(jnp.int32, (own, HEAD), 1)
    mine = jnp.zeros((own, HEAD), f32)
    for h in range(heads):
        cols = slice(h * HEAD, (h + 1) * HEAD)
        mine = jnp.where(spot == h, jnp.sum(q[:, cols] * kn[:, cols], axis=1, keepdims=True), mine)
    loads[4].wait()
    loads[5].wait()
    for k, piece in enumerate(pieces(tok[...].astype(f32))):
        tp[k] = piece
    gains = jnp.concatenate(
        [
            jnp.broadcast_to(gain[:, b * width : (b + 1) * width], (few, width)) for b in range(t)
        ],
        axis=0,
    )
    got[me] = part[me]
    take()
    coded = got[:, :, width:].astype(f32)
    stat = (coded + pltpu.roll(coded, HEAD - kinds, axis=2)) + pltpu.roll(
        coded, HEAD - 2 * kinds, axis=2
    )
    top = jnp.maximum(jnp.max(stat, axis=0), mine)
    scale = jnp.exp(stat - top[None])
    mass = pltpu.roll(stat, HEAD - heads, axis=2)
    self_w = jnp.exp(mine - top)
    total = self_w + jnp.sum(scale * mass, axis=0)
    attended = []
    for h in range(heads):
        cols = slice(h * HEAD, (h + 1) * HEAD)
        older = jnp.sum(got[:, :, cols].astype(f32) * scale[:, :, h : h + 1], axis=0)
        attended.append((self_w[:, h : h + 1] * vn[:, cols] + older) / total[:, h : h + 1])
    attended = jnp.concatenate(attended, axis=1).astype(b16)
    loads[6].wait()
    for k, piece in enumerate(pieces(dot(attended, wo[...]))):
        zs[k] = piece.astype(b16)
    send, take = z_copies(lambda peer: zs.at[peer], zr, z_s, z_r)
    send()
    mid = zs[z].astype(f32)
    take()
    for i in range(1, t):
        mid += zr[lax.rem(z + i, t)].astype(f32)
    mid += tp[z]
    for copy in up_relay:
        copy.start()
    for copy in down_side:
        copy.wait()
    for copy in down_relay:
        copy.start()

    def mean(a):
        r = jnp.broadcast_to(jnp.sum(a, axis=1, keepdims=True), (own, HEAD))
        whole = r
        for b in range(1, t):
            whole += pltpu.roll(r, b * few, axis=0)
        return whole[:, :1] / wide

    shifted = mid - mean(mid)
    normed = (shifted * lax.rsqrt(mean(shifted * shifted) + 1e-05) * gains).astype(b16)
    ns[...] = normed
    nr[me] = normed
    send, take = line_copies(lambda peer: ns, nr, n_s, n_r)
    send()
    for i in (0, 2, 3):
        loads[i].wait()
    for copy in up_side + up_relay:
        copy.wait()
    take()
    rows, units = n * own, t * up.shape[0]
    row_block = lax.rem(lax.broadcasted_iota(jnp.int32, (rows, width), 0), own) // few
    x = nr[...].astype(f32).reshape(rows, width).astype(b16)
    pre = jnp.zeros((rows, units), f32)
    for b in range(t):
        y = lax.dot_general(
            x, upb[:, :, b * width : (b + 1) * width].reshape(units, width), NT,
            preferred_element_type=f32,
        )
        pre = jnp.where(row_block[:, :units] == b, y, pre)
    pre = pre.reshape(n, own, units)
    whole = pre
    for b in range(1, t):
        whole += pltpu.roll(pre, b * few, axis=1)
    act = (0.5 * whole * (1.0 + lax.erf(whole * 0.5**0.5))).reshape(rows, units).astype(b16)
    loads[1].wait()
    for copy in down_relay:
        copy.wait()
    term = jnp.zeros((rows, width), f32)
    for b in range(t):
        y = dot(act, dnb[:, :, b * width : (b + 1) * width].reshape(units, width))
        term = jnp.where(row_block == b, y, term)
    term = term.reshape(n, own, width).astype(b16)
    ts[...] = term
    send, take = line_copies(lambda peer: ts.at[peer], rr, r_s, r_r)
    send()
    rr[me] = ts[me]
    take()
    out = (mid + jnp.sum(rr[...].astype(f32), axis=0)).astype(b16)
    fs[...] = out
    fr[z] = out
    send, take = z_copies(lambda peer: fs, fr, f_s, f_r)
    send()
    take()
    every = [fr[k].astype(f32) for k in range(t)]
    final = jnp.zeros((own, width), f32)
    for b in range(t):
        rows_b = jnp.concatenate([a[b * few : (b + 1) * few] for a in every], axis=0)
        final = jnp.where(z == b, rows_b, final)
    hid[...] = final.astype(b16)
    for copies in sent:
        copies.wait_send()


def body(
    n, t, tokens, first_gain, query_weight, key_weight, value_weight, out_weight, second_gain,
    up_weight, down_weight, cache_keys, cache_values, lengths, stream_order,
):
    f32, b16 = jnp.float32, jnp.bfloat16
    own, wide = tokens.shape
    width = query_weight.shape[1]
    requests = own * n
    units = up_weight.shape[1]
    rows = cache_keys.shape[0]
    steps = rows // CHUNK
    vmem = pl.BlockSpec(memory_space=pltpu.VMEM)
    hbm = pl.BlockSpec(memory_space=pltpu.HBM)
    dma = pltpu.SemaphoreType.DMA
    shape = jax.ShapeDtypeStruct
    up_rows = up_weight.T
    held = lambda a: pltpu.with_memory_space_constraint(a, pltpu.HBM)
    heads = width // HEAD
    q_all, nk, nv, tab, kb, vb, un = pl.pallas_call(
        functools.partial(project, n, t),
        out_shape=(
            shape((n, own, width), b16),
            shape((own, width), b16),
            shape((own, width), b16),
            shape((8, requests), f32),
            shape((rows, width), b16),
            shape((rows, width), b16),
            shape((2, units // 2, wide), b16),
        ),
        in_specs=[hbm] * 10,
        out_specs=(vmem,) * 7,
        scratch_shapes=[
            pltpu.VMEM((own, wide), b16),
            pltpu.VMEM((1, wide), f32),
            pltpu.VMEM((1, requests), jnp.int32),
            pltpu.VMEM((1, requests), jnp.int32),
            pltpu.VMEM((3, wide, width), b16),
            pltpu.VMEM((own, width), b16),
            dma((12,)),
            dma((1,)), dma((1,)),
            dma((2,)), dma((2,)),
        ],
        compiler_params=pltpu.CompilerParams(
            collective_id=0, has_side_effects=True, vmem_limit_bytes=VMEM_PROJECT
        ),
        name="project",
    )(
        *map(
            held,
            (
                tokens, first_gain.reshape(1, wide), lengths.reshape(1, requests),
                stream_order.reshape(1, requests), query_weight, key_weight, value_weight,
                cache_keys, cache_values, up_rows,
            ),
        )
    )
    more, new_keys, new_values = pl.pallas_call(
        further,
        out_shape=(
            shape((requests, width + HEAD), f32),
            shape((own, width), b16),
            shape((own, width), b16),
        ),
        in_specs=[vmem] * 6,
        out_specs=(vmem,) * 3,
        scratch_shapes=[
            pltpu.VMEM((WIN * heads, rows), f32),
            pltpu.VMEM((WIN * heads, width), f32),
        ],
        compiler_params=pltpu.CompilerParams(vmem_limit_bytes=VMEM_FURTHER),
        name="further",
    )(q_all, tab, nk, nv, kb, vb)
    hidden = pl.pallas_call(
        functools.partial(tail, n, t),
        out_shape=shape((own, width), b16),
        in_specs=[vmem] * 8 + [hbm] * 5,
        out_specs=vmem,
        scratch_shapes=[
            pltpu.VMEM((WIN * heads, rows), f32),
            pltpu.VMEM((WIN * heads, width), f32),
            pltpu.VMEM((n, own, width + HEAD), b16),
            pltpu.VMEM((own, wide), b16),
            pltpu.VMEM((1, wide), f32),
            pltpu.VMEM((width, wide), b16),
            pltpu.VMEM((n, own, width + HEAD), b16),
            pltpu.VMEM((t, units, wide), b16),
            pltpu.VMEM((t, units, wide), b16),
            pltpu.VMEM((t, own, width), b16),
            pltpu.VMEM((t, own, width), b16),
            pltpu.VMEM((t, own, width), f32),
            pltpu.VMEM((own, width), b16),
            pltpu.VMEM((n, own, width), b16),
            pltpu.VMEM((n, own, width), b16),
            pltpu.VMEM((n, own, width), b16),
            pltpu.VMEM((own, width), b16),
            pltpu.VMEM((t, own, width), b16),
            dma((7,)),
            dma((1,)), dma((1,)),
            dma((2,)), dma((2,)),
            dma((2,)), dma((2,)),
            dma((2,)), dma((2,)),
            dma((2,)), dma((2,)),
            dma((1,)), dma((1,)),
            dma((1,)), dma((1,)),
            dma((1,)), dma((1,)),
            dma((1,)), dma((1,)),
        ],
        compiler_params=pltpu.CompilerParams(
            collective_id=1, has_side_effects=True, vmem_limit_bytes=VMEM_TAIL
        ),
        name="tail",
    )(
        more, q_all, tab, kb, vb, nk, nv, un,
        *map(held, (tokens, second_gain.reshape(1, wide), out_weight, up_rows, down_weight)),
    )
    return hidden, new_keys, new_values


def solution(mesh):
    n, t = mesh.shape["req"], mesh.shape["tp"]
    return jax.shard_map(
        functools.partial(body, n, t),
        mesh=mesh,
        in_specs=(
            P("req", None), P(), P(None, "tp"), P(None, "tp"), P(None, "tp"), P("tp", None), P(),
            P(None, ("req", "tp")), P(("req", "tp"), None), P("req", "tp"), P("req", "tp"), P(), P(),
        ),
        out_specs=(P("req", "tp"), P("req", "tp"), P("req", "tp")),
        check_vma=False,
    )
```
